256 devices in a mesh: dp: 8 (over z_hi, x), expert: 32 (over z_lo, y, core).
Axes of the slice: x: 4, y: 4, z: 8 (z_hi: 2, z_lo: 4; z = z_hi * 4 + z_lo), core: 2. Of those that a mesh axis runs over, the one named last changes fastest.
Arguments:
- tokens: bfloat16 [32768, 3584], P(('dp', 'expert')), may hold values from -6 to 6
- cotangent: bfloat16 [32768, 3584], P(('dp', 'expert')), may hold values from -0.09375 to 0.09375
- expert_ids: int32 [32768, 8], P(('dp', 'expert')), may hold values from 0 to 255, all different within a row; in each aligned block of 128 rows (0 to 127, 128 to 255, ...) at most 6 rows name the same one
- gates: bfloat16 [32768, 8], P(('dp', 'expert')), may hold values from 0.049804688 to 1
- swap_flags: int32 [16], replicated, may hold values 0 or 1
- gate_w: bfloat16 [32, 3584, 1024], P('expert', None, 'dp'), may hold values from -0.09375 to 0.09375
- up_w: bfloat16 [32, 3584, 1024], P('expert', None, 'dp'), may hold values from -0.09375 to 0.09375
- down_w: bfloat16 [32, 1024, 3584], P('expert', 'dp'), may hold values from -0.1875 to 0.1875
Outputs:
- grad_gate_w: bfloat16 [32, 3584, 1024], P('expert', None, 'dp')
- grad_up_w: bfloat16 [32, 3584, 1024], P('expert', None, 'dp')
- grad_down_w: bfloat16 [32, 1024, 3584], P('expert', 'dp')
- score_grad: float32 [32768, 8], P(('dp', 'expert'))
The draws below stay inside these ranges and needn't reach their ends.
Inputs may be any that keep to these rules, and one draw needn't show every extreme that they name: `expert_ids`: among the 128 rows of one device no expert is named more than 6 times, a bound that some block reaches; the numbers of one row differ. `swap_flags`: 1 means that slots s and s + 16 trade their experts.
All inputs are finite; a program needn't handle non-finite values.
Results may differ from the reference program's by a relative error of at most 0.011.
Values may be sent and summed in bfloat16 or wider, within the bound.
A program may use at most 128 MiB of HBM per device.

```python
import math
import jax
import jax.numpy as jnp
import numpy as np
from jax import lax

D = 3584
F = 1024
ALL_EXPERTS = 256
TOPK = 8
TOK_DEV = 128
CAP = 6
EXPERTS = 32
HALF = 16
TOKENS = 32768
N_DP = 8
N_EXPERT = 32


def with_ends(array, stream_key, least, largest):
    dims = array.shape
    index_at = [jax.random.randint(jax.random.fold_in(stream_key, axis), (), 0, dims[axis]) for axis in range(len(dims))]
    array = array.at[tuple(index_at)].set(least)
    longest = dims.index(max(dims))
    index_at[longest] = (index_at[longest] + 1) % dims[longest]
    return array.at[tuple(index_at)].set(largest)


def block_scale(key, extent, cuts, least, high):
    gain = 1.0
    for position, shards_of in cuts:
        draws = jax.random.uniform(jax.random.fold_in(jax.random.fold_in(key, 6), position), (shards_of,), jnp.float32, least / len(cuts), high / len(cuts))
        gain = gain * jnp.repeat(jnp.exp(draws), extent[position] // shards_of).reshape((-1,) + (1,) * (len(extent) - 1 - position))
    return gain


def assign_block(own_key, own, number, rows, amount, top, bound, skew):
    order = jax.random.permutation(own_key, amount)
    crowded, usual = shares(amount, rows * top, bound, skew, True), shares(amount, rows * top, bound, skew, False)
    places = jnp.arange(amount)

    def named(lengths, turn):
        used = int((lengths > 0).sum())
        fixed = max(1, used // 4)
        moved = fixed + (places - fixed + turn * (used - fixed)) % max(1, amount - fixed)
        return jnp.zeros((amount,), jnp.int32).at[order[jnp.where(places < fixed, places, moved)]].set(jnp.asarray(lengths, jnp.int32))

    lengths = jnp.where(number % 4 == 0, named(crowded, number // 4), named(usual, number - number // 4 - 1))
    mixed = jax.random.permutation(jax.random.fold_in(own, 3), amount)
    donor, taker = mixed[0:amount // 2 * 2:2], mixed[1:amount // 2 * 2:2]
    slack = jnp.minimum(lengths[donor] - 1, bound - lengths[taker]) // 2
    slack = jnp.where((donor == order[0]) | (taker == order[0]) | (lengths[taker] == 0), 0, jnp.maximum(slack, 0))
    moved = jax.random.randint(jax.random.fold_in(own, 4), (amount // 2,), 0, 1 << 20) % (slack + 1)
    lengths = lengths.at[donor].add(-moved).at[taker].add(moved)
    members = jnp.searchsorted(jnp.cumsum(lengths), jnp.arange(rows * top), side="right").astype(jnp.int32)
    grid = members.reshape(top, rows).T
    grid = grid[jax.random.permutation(jax.random.fold_in(own, 1), rows)]
    turn = jax.random.randint(jax.random.fold_in(own, 2), (rows, 1), 0, top)
    return jnp.take_along_axis(grid, (jnp.arange(top)[None, :] + turn) % top, axis=1)


def shares(count, total, bound, slope, full):
    portions = [(1 << 20) // math.isqrt(standing ** slope) + 1 for standing in range(1, count + 1)]
    largest = bound if full else min(bound, max(-(-total // count), total * portions[0] // sum(portions)))
    least = 1 if total - largest >= count - 1 else 0
    holding, rest = [largest] + [least] * (count - 1), total - largest - least * (count - 1)
    while rest > 0:
        free = [i for i in range(1, count) if holding[i] < largest] or [i for i in range(1, count) if holding[i] < bound]
        pool, budget = sum([portions[i] for i in free]), rest
        for i in free:
            more = min(bound - holding[i], max(1, budget * portions[i] // pool), rest)
            holding[i] = holding[i] + more
            rest = rest - more
    return np.array(holding)


def centred(rng, dims, scale, bound, split=(), held_as=jnp.bfloat16):
    level = block_scale(rng, dims, split, -0.22, 0.18) if split else 1.0
    array = jax.random.normal(rng, dims, jnp.float32) * scale * level
    return jnp.minimum(jnp.maximum(array, -bound), bound).astype(held_as)


def setup_inputs(seed: int = 0) -> dict:
    streams_of = jax.random.split(jax.random.key(seed), 9)
    tokens = centred(streams_of[0], (TOKENS, D), 1.0, 6.0, ((0, 256),))
    cotangent = centred(streams_of[1], (TOKENS, D), D ** -0.5, 0.09375, ((0, 256),))
    expert_ids_keys = jax.random.split(jax.random.fold_in(streams_of[2], 1), TOKENS // TOK_DEV)
    expert_ids_turns = jax.random.permutation(jax.random.fold_in(streams_of[2], 3), TOKENS // TOK_DEV)
    expert_ids = jax.vmap(lambda own, number: assign_block(jax.random.fold_in(streams_of[2], 2), own, number, TOK_DEV, ALL_EXPERTS, TOPK, CAP, 2))(expert_ids_keys, expert_ids_turns).reshape((TOKENS, TOPK))
    gates = jnp.clip(jnp.exp(math.log(1.0) - 2.9996462 * jax.random.uniform(streams_of[3], (TOKENS, TOPK), jnp.float32) ** block_scale(streams_of[3], (TOKENS, TOPK), ((0, 256),), -0.2, 0.2)), 0.049804688, 1.0).astype(jnp.bfloat16)
    swap_flags = with_ends((jax.random.randint(streams_of[4], (HALF,), 0, 2) < 1).astype(jnp.int32), jax.random.fold_in(streams_of[4], 1), 0, 1)
    gate_w = centred(streams_of[5], (EXPERTS, D, F), D ** -0.5, 0.09375, ((0, 32), (2, 8)))
    up_w = centred(streams_of[6], (EXPERTS, D, F), D ** -0.5, 0.09375, ((0, 32), (2, 8)))
    down_w = centred(streams_of[7], (EXPERTS, F, D), F ** -0.5, 0.1875, ((0, 32), (1, 8)))
    return {"tokens": tokens, "cotangent": cotangent, "expert_ids": expert_ids, "gates": gates, "swap_flags": swap_flags, "gate_w": gate_w, "up_w": up_w, "down_w": down_w}


def reference(tokens, cotangent, expert_ids, gates, swap_flags, gate_w, up_w, down_w):
    most_rows = CAP * N_DP * N_EXPERT
    flat_ids = expert_ids.reshape(-1).astype(jnp.int32)
    choice_count = flat_ids.shape[0]
    valid = flat_ids < EXPERTS
    sort_keys = jnp.where(valid, flat_ids, EXPERTS).astype(jnp.int32)
    order = jnp.argsort(sort_keys, stable=True).astype(jnp.int32)
    counts = jnp.sum(jnp.where(sort_keys[:, None] == jnp.arange(EXPERTS, dtype=jnp.int32)[None, :], 1, 0), axis=0).astype(jnp.int32)
    starts = (jnp.cumsum(counts) - counts).astype(jnp.int32)
    order_pad = jnp.concatenate([order, jnp.zeros((most_rows,), jnp.int32)])
    flat_gates = gates.reshape(-1)
    contract = (((0,), (0,)), ((), ()))

    def one_expert(expert):
        index = lax.dynamic_slice_in_dim(order_pad, starts[expert], most_rows)
        live = jnp.arange(most_rows, dtype=jnp.int32) < counts[expert]
        token_index = (index // TOPK).astype(jnp.int32)
        row_x = jnp.where(live[:, None], tokens[token_index], jnp.zeros((), tokens.dtype))
        row_dy = jnp.where(live[:, None], cotangent[token_index], jnp.zeros((), cotangent.dtype))
        row_g = jnp.where(live, flat_gates[index], jnp.zeros((), gates.dtype)).reshape(-1, 1)
        w_gate = gate_w[expert]
        w_up = up_w[expert]
        w_down = down_w[expert]
        pre_gate = jnp.dot(row_x, w_gate, preferred_element_type=jnp.float32)
        pre_up = jnp.dot(row_x, w_up, preferred_element_type=jnp.float32)
        sigma = jax.nn.sigmoid(pre_gate)
        active = pre_gate * sigma
        hidden = (active * pre_up).astype(jnp.bfloat16)
        back = lax.dot_general(row_dy, w_down, (((1,), (1,)), ((), ())), preferred_element_type=jnp.float32)
        score = jnp.sum(hidden.astype(jnp.float32) * back, axis=1)
        scaled = row_dy * row_g
        d_hidden = row_g.astype(jnp.float32) * back
        d_gate = (d_hidden * pre_up * sigma * (1.0 + pre_gate * (1.0 - sigma))).astype(jnp.bfloat16)
        d_up = (d_hidden * active).astype(jnp.bfloat16)
        grad_gate = lax.dot_general(row_x, d_gate, contract, preferred_element_type=jnp.float32)
        grad_up = lax.dot_general(row_x, d_up, contract, preferred_element_type=jnp.float32)
        grad_down = lax.dot_general(hidden, scaled, contract, preferred_element_type=jnp.float32)
        places = jnp.where(live, index, choice_count).astype(jnp.int32)
        return (grad_gate.astype(jnp.bfloat16), grad_up.astype(jnp.bfloat16), grad_down.astype(jnp.bfloat16), score, places)

    grads_gate, grads_up, grads_down, scores, places = lax.map(one_expert, jnp.arange(EXPERTS, dtype=jnp.int32))
    score_flat = jnp.zeros((choice_count + 1,), jnp.float32).at[places.reshape(-1)].set(scores.reshape(-1).astype(jnp.float32))
    score_grad = score_flat[:choice_count].reshape(expert_ids.shape)
    slot_ids = jnp.arange(EXPERTS, dtype=jnp.int32)
    holder = jnp.where(swap_flags[slot_ids % HALF] == 1, jnp.bitwise_xor(slot_ids, HALF), slot_ids).astype(jnp.int32)
    return (grads_gate[holder], grads_up[holder], grads_down[holder], score_grad)
```

```python
import jax
import jax.numpy as jnp
from jax import lax
from jax.sharding import PartitionSpec as P

CAP = 6
LANE = 128


def partner(block, axis, stride):
    count = lax.axis_size(axis)
    route = []
    for low in range(count):
        high = low | 1 << stride
        if high != low and high < count:
            route += [(low, high), (high, low)]
    return lax.ppermute(block, axis, route)


def body(tokens, cotangent, expert_ids, gates, swap_flags, gate_w, up_w, down_w):
    axis_len = lax.axis_size("expert")
    half_axis = axis_len // 2
    pair_bit = axis_len.bit_length() - 2
    own_slot = lax.axis_index("expert")
    tok_count = tokens.shape[0]
    top_count = expert_ids.shape[1]
    width = tokens.shape[1]
    flat_ids = expert_ids.reshape(-1)
    choice_count = flat_ids.shape[0]
    valid = flat_ids < axis_len
    pair_index = jnp.arange(half_axis, dtype=jnp.int32)
    flag_of = jnp.sum(
        jnp.where((flat_ids % half_axis)[:, None] == pair_index[None, :], swap_flags[None, :], 0),
        axis=1,
    )
    own_flag = jnp.sum(jnp.where(pair_index == own_slot % half_axis, swap_flags, 0))
    target = jnp.where(flag_of == 1, jnp.bitwise_xor(flat_ids, half_axis), flat_ids)
    target = jnp.where(valid, target, 0)
    onehot = jnp.where(
        (target[:, None] == jnp.arange(axis_len, dtype=jnp.int32)[None, :]) & valid[:, None], 1, 0
    ).astype(jnp.int32)
    ranks = jnp.sum(jnp.cumsum(onehot, axis=0) * onehot, axis=1) - 1
    slot_count = axis_len * CAP
    slots = jnp.where(valid, target * CAP + ranks, slot_count)
    source = (
        jnp.full((slot_count,), choice_count, jnp.int32)
        .at[slots]
        .set(jnp.arange(choice_count, dtype=jnp.int32), mode="drop")
    )
    token_index = source // top_count
    padded_x = jnp.concatenate([tokens, jnp.zeros((1, width), tokens.dtype)], axis=0)
    padded_dy = jnp.concatenate([cotangent, jnp.zeros((1, width), cotangent.dtype)], axis=0)
    padded_g = jnp.concatenate([gates.reshape(-1), jnp.zeros((1,), gates.dtype)], axis=0)
    send_g = padded_g[source]
    g_cols = jnp.where(
        jnp.arange(LANE, dtype=jnp.int32)[None, :] == 0, send_g[:, None], jnp.zeros((), gates.dtype)
    )
    packed = jnp.concatenate([padded_x[token_index], padded_dy[token_index], g_cols], axis=1)
    row_width = packed.shape[1]
    packed = packed.reshape(axis_len, CAP, row_width)
    recv = lax.all_to_all(packed, "expert", split_axis=0, concat_axis=0, tiled=True)
    w_gate = gate_w[0]
    w_up = up_w[0]
    w_down = down_w[0]
    other_gate, other_up, other_down = partner((gate_w, up_w, down_w), "expert", pair_bit)
    taken = own_flag == 1
    w_gate = jnp.where(taken, other_gate[0], w_gate)
    w_up = jnp.where(taken, other_up[0], w_up)
    w_down = jnp.where(taken, other_down[0], w_down)
    contract = (((0,), (0,)), ((), ()))
    gathered = lax.all_gather(recv, "dp", axis=0, tiled=True)
    block_count = lax.axis_size("dp")
    rows = gathered.reshape(-1, row_width)
    row_x = rows[:, :width]
    row_dy = rows[:, width:2 * width]
    row_g = rows[:, 2 * width:2 * width + 1]
    pre_gate = jnp.dot(row_x, w_gate, preferred_element_type=jnp.float32)
    pre_up = jnp.dot(row_x, w_up, preferred_element_type=jnp.float32)
    sigma = jax.nn.sigmoid(pre_gate)
    active = pre_gate * sigma
    hidden = (active * pre_up).astype(jnp.bfloat16)
    back = lax.dot_general(
        row_dy, w_down, (((1,), (1,)), ((), ())), preferred_element_type=jnp.float32
    )
    score = jnp.sum(hidden.astype(jnp.float32) * back, axis=1)
    scaled = row_dy * row_g
    d_hidden = row_g.astype(jnp.float32) * back
    d_gate = (d_hidden * pre_up * sigma * (1.0 + pre_gate * (1.0 - sigma))).astype(jnp.bfloat16)
    d_up = (d_hidden * active).astype(jnp.bfloat16)
    grad_gate = lax.dot_general(row_x, d_gate, contract, preferred_element_type=jnp.float32)
    grad_up = lax.dot_general(row_x, d_up, contract, preferred_element_type=jnp.float32)
    grad_down = lax.dot_general(hidden, scaled, contract, preferred_element_type=jnp.float32)
    scores = score.reshape(block_count, axis_len, CAP)
    own_scores = lax.psum_scatter(scores, "dp", scatter_dimension=0, tiled=True)
    own_scores = own_scores.reshape(axis_len, CAP)
    returned = lax.all_to_all(own_scores, "expert", split_axis=0, concat_axis=0, tiled=True)
    picked = returned.reshape(-1)[jnp.minimum(slots, slot_count - 1)]
    score_grad = jnp.where(valid, picked, 0.0).reshape(tok_count, top_count)
    out_gate = grad_gate.astype(jnp.bfloat16)[None]
    out_up = grad_up.astype(jnp.bfloat16)[None]
    out_down = grad_down.astype(jnp.bfloat16)[None]
    return (out_gate, out_up, out_down, score_grad)


def solution(mesh):
    placed = (
        P(("dp", "expert"), None),
        P(("dp", "expert"), None),
        P(("dp", "expert"), None),
        P(("dp", "expert"), None),
        P(),
        P("expert", None, "dp"),
        P("expert", None, "dp"),
        P("expert", "dp", None),
    )
    return jax.shard_map(
        body,
        mesh=mesh,
        in_specs=placed,
        out_specs=(
            P("expert", None, "dp"),
            P("expert", None, "dp"),
            P("expert", "dp", None),
            P(("dp", "expert"), None),
        ),
        check_vma=False,
    )
```

```python
import jax
import jax.numpy as jnp
from jax import lax
from jax.sharding import PartitionSpec as P

CAP = 6
LANE = 128


def partner(block, axis, stride):
    count = lax.axis_size(axis)
    route = []
    for low in range(count):
        high = low | 1 << stride
        if high != low and high < count:
            route += [(low, high), (high, low)]
    return lax.ppermute(block, axis, route)


def body(tokens, cotangent, expert_ids, gates, swap_flags, gate_w, up_w, down_w):
    axis_len = lax.axis_size("expert")
    half_axis = axis_len // 2
    pair_bit = axis_len.bit_length() - 2
    own_slot = lax.axis_index("expert")
    tok_count = tokens.shape[0]
    top_count = expert_ids.shape[1]
    width = tokens.shape[1]
    flat_ids = expert_ids.reshape(-1)
    choice_count = flat_ids.shape[0]
    valid = flat_ids < axis_len
    pair_index = jnp.arange(half_axis, dtype=jnp.int32)
    flag_of = jnp.sum(
        jnp.where((flat_ids % half_axis)[:, None] == pair_index[None, :], swap_flags[None, :], 0),
        axis=1,
    )
    own_flag = jnp.sum(jnp.where(pair_index == own_slot % half_axis, swap_flags, 0))
    target = jnp.where(flag_of == 1, jnp.bitwise_xor(flat_ids, half_axis), flat_ids)
    target = jnp.where(valid, target, 0)
    onehot = jnp.where(
        (target[:, None] == jnp.arange(axis_len, dtype=jnp.int32)[None, :]) & valid[:, None], 1, 0
    ).astype(jnp.int32)
    ranks = jnp.sum(jnp.cumsum(onehot, axis=0) * onehot, axis=1) - 1
    slot_count = axis_len * CAP
    slots = jnp.where(valid, target * CAP + ranks, slot_count)
    source = (
        jnp.full((slot_count,), choice_count, jnp.int32)
        .at[slots]
        .set(jnp.arange(choice_count, dtype=jnp.int32), mode="drop")
    )
    token_index = source // top_count
    padded_x = jnp.concatenate([tokens, jnp.zeros((1, width), tokens.dtype)], axis=0)
    padded_dy = jnp.concatenate([cotangent, jnp.zeros((1, width), cotangent.dtype)], axis=0)
    padded_g = jnp.concatenate([gates.reshape(-1), jnp.zeros((1,), gates.dtype)], axis=0)
    send_g = padded_g[source]
    g_cols = jnp.where(
        jnp.arange(LANE, dtype=jnp.int32)[None, :] == 0, send_g[:, None], jnp.zeros((), gates.dtype)
    )
    packed = jnp.concatenate([padded_x[token_index], padded_dy[token_index], g_cols], axis=1)
    row_width = packed.shape[1]
    packed = packed.reshape(axis_len, CAP, row_width)
    recv = lax.all_to_all(packed, "expert", split_axis=0, concat_axis=0, tiled=True)
    w_gate = gate_w[0]
    w_up = up_w[0]
    w_down = down_w[0]
    other_gate, other_up, other_down = partner((gate_w, up_w, down_w), "expert", pair_bit)
    taken = own_flag == 1
    w_gate = jnp.where(taken, other_gate[0], w_gate)
    w_up = jnp.where(taken, other_up[0], w_up)
    w_down = jnp.where(taken, other_down[0], w_down)
    gathered = lax.all_gather(recv, "dp", axis=0, tiled=True)
    block_count = lax.axis_size("dp")
    row_x = gathered[:, :, :width]
    row_dy = gathered[:, :, width:2 * width]
    row_g = gathered[:, :, 2 * width:2 * width + 1]
    feature = (((2,), (0,)), ((), ()))
    rows_contract = (((0, 1), (0, 1)), ((), ()))
    pre_gate = lax.dot_general(row_x, w_gate, feature, preferred_element_type=jnp.float32)
    pre_up = lax.dot_general(row_x, w_up, feature, preferred_element_type=jnp.float32)
    sigma = jax.nn.sigmoid(pre_gate)
    active = pre_gate * sigma
    hidden = (active * pre_up).astype(jnp.bfloat16)
    back = lax.dot_general(
        row_dy, w_down, (((2,), (1,)), ((), ())), preferred_element_type=jnp.float32
    )
    score = jnp.sum(hidden.astype(jnp.float32) * back, axis=2)
    scaled = row_dy * row_g
    d_hidden = row_g.astype(jnp.float32) * back
    d_gate = (d_hidden * pre_up * sigma * (1.0 + pre_gate * (1.0 - sigma))).astype(jnp.bfloat16)
    d_up = (d_hidden * active).astype(jnp.bfloat16)
    grad_gate = lax.dot_general(row_x, d_gate, rows_contract, preferred_element_type=jnp.float32)
    grad_up = lax.dot_general(row_x, d_up, rows_contract, preferred_element_type=jnp.float32)
    grad_down = lax.dot_general(hidden, scaled, rows_contract, preferred_element_type=jnp.float32)
    scores = score.reshape(block_count, axis_len * CAP)
    parts = lax.all_to_all(scores, "dp", split_axis=0, concat_axis=0, tiled=True)
    own_scores = jnp.sum(parts, axis=0).reshape(axis_len, CAP)
    returned = lax.all_to_all(own_scores, "expert", split_axis=0, concat_axis=0, tiled=True)
    picked = returned.reshape(-1)[jnp.minimum(slots, slot_count - 1)]
    score_grad = jnp.where(valid, picked, 0.0).reshape(tok_count, top_count)
    out_gate = grad_gate.astype(jnp.bfloat16)[None]
    out_up = grad_up.astype(jnp.bfloat16)[None]
    out_down = grad_down.astype(jnp.bfloat16)[None]
    return (out_gate, out_up, out_down, score_grad)


def solution(mesh):
    placed = (
        P(("dp", "expert"), None),
        P(("dp", "expert"), None),
        P(("dp", "expert"), None),
        P(("dp", "expert"), None),
        P(),
        P("expert", None, "dp"),
        P("expert", None, "dp"),
        P("expert", "dp", None),
    )
    return jax.shard_map(
        body,
        mesh=mesh,
        in_specs=placed,
        out_specs=(
            P("expert", None, "dp"),
            P("expert", None, "dp"),
            P("expert", "dp", None),
            P(("dp", "expert"), None),
        ),
        check_vma=False,
    )
```

```python
import functools

import jax
import jax.numpy as jnp
from jax import lax
from jax.experimental import pallas as pl
from jax.experimental.pallas import tpu as pltpu
from jax.sharding import PartitionSpec as P

CAP = 6
LANE = 128


def partner(block, axis, stride):
    count = lax.axis_size(axis)
    route = []
    for low in range(count):
        high = low | 1 << stride
        if high != low and high < count:
            route += [(low, high), (high, low)]
    return lax.ppermute(block, axis, route)


def dp_gather_kernel(n_dp, ring, x_ref, o_ref, recv, send):
    me = lax.axis_index("dp")
    ex = lax.axis_index("expert")
    rows = x_ref.shape[0]
    half = rows // 2
    plane = me // ring
    pos = me % ring
    left = plane * ring + (pos + ring - 1) % ring
    right = plane * ring + (pos + 1) % ring
    far = plane * ring + (pos + 2) % ring
    across = (me + ring) % n_dp

    def block(k):
        return o_ref.at[pl.ds(k * rows, rows)]

    def part(k, i):
        return o_ref.at[pl.ds(k * rows + i * half, half)]

    def push(src, dst, slot, k, peer):
        copy = pltpu.make_async_remote_copy(
            src_ref=src,
            dst_ref=dst,
            send_sem=send.at[slot],
            recv_sem=recv.at[k],
            device_id=(peer, ex),
            device_id_type=pl.DeviceIdType.MESH,
        )
        copy.start()
        return copy

    def arrived(k):
        pltpu.make_async_copy(block(k), block(k), recv.at[k]).wait()

    barrier = pltpu.get_barrier_semaphore()
    for peer in (left, right, across):
        pl.semaphore_signal(barrier, inc=1, device_id=(peer, ex), device_id_type=pl.DeviceIdType.MESH)
    pl.semaphore_wait(barrier, 3)

    local = pltpu.make_async_copy(x_ref, block(me), recv.at[me])
    local.start()
    sent = [
        push(x_ref, block(me), 0, me, across),
        push(x_ref, block(me), 1, me, left),
        push(x_ref, block(me), 2, me, right),
    ]
    arrived(left)
    sent.append(push(part(left, 0), part(left, 0), 3, left, right))
    arrived(right)
    sent.append(push(part(right, 1), part(right, 1), 4, right, left))
    arrived(across)
    sent.append(push(block(across), block(across), 5, across, left))
    sent.append(push(block(across), block(across), 6, across, right))
    left_across = (left + ring) % n_dp
    right_across = (right + ring) % n_dp
    arrived(left_across)
    sent.append(push(part(left_across, 0), part(left_across, 0), 7, left_across, right))
    arrived(right_across)
    sent.append(push(part(right_across, 1), part(right_across, 1), 8, right_across, left))
    arrived(far)
    arrived((far + ring) % n_dp)
    local.wait()
    for copy in sent:
        copy.wait_send()


def dp_gather(block):
    n_dp = lax.axis_size("dp")
    ring = n_dp // 2
    rows = block.shape[0]
    return pl.pallas_call(
        functools.partial(dp_gather_kernel, n_dp, ring),
        out_shape=jax.ShapeDtypeStruct((n_dp * rows,) + block.shape[1:], block.dtype),
        in_specs=[pl.BlockSpec(memory_space=pl.ANY)],
        out_specs=pl.BlockSpec(memory_space=pl.ANY),
        scratch_shapes=[pltpu.SemaphoreType.DMA((n_dp,)), pltpu.SemaphoreType.DMA((9,))],
        compiler_params=pltpu.CompilerParams(collective_id=0, has_side_effects=True),
    )(block)


def body(tokens, cotangent, expert_ids, gates, swap_flags, gate_w, up_w, down_w):
    axis_len = lax.axis_size("expert")
    half_axis = axis_len // 2
    pair_bit = axis_len.bit_length() - 2
    own_slot = lax.axis_index("expert")
    tok_count = tokens.shape[0]
    top_count = expert_ids.shape[1]
    width = tokens.shape[1]
    flat_ids = expert_ids.reshape(-1)
    choice_count = flat_ids.shape[0]
    valid = flat_ids < axis_len
    pair_index = jnp.arange(half_axis, dtype=jnp.int32)
    flag_of = jnp.sum(
        jnp.where((flat_ids % half_axis)[:, None] == pair_index[None, :], swap_flags[None, :], 0),
        axis=1,
    )
    own_flag = jnp.sum(jnp.where(pair_index == own_slot % half_axis, swap_flags, 0))
    target = jnp.where(flag_of == 1, jnp.bitwise_xor(flat_ids, half_axis), flat_ids)
    target = jnp.where(valid, target, 0)
    onehot = jnp.where(
        (target[:, None] == jnp.arange(axis_len, dtype=jnp.int32)[None, :]) & valid[:, None], 1, 0
    ).astype(jnp.int32)
    ranks = jnp.sum(jnp.cumsum(onehot, axis=0) * onehot, axis=1) - 1
    slot_count = axis_len * CAP
    slots = jnp.where(valid, target * CAP + ranks, slot_count)
    source = (
        jnp.full((slot_count,), choice_count, jnp.int32)
        .at[slots]
        .set(jnp.arange(choice_count, dtype=jnp.int32), mode="drop")
    )
    token_index = source // top_count
    padded_x = jnp.concatenate([tokens, jnp.zeros((1, width), tokens.dtype)], axis=0)
    padded_dy = jnp.concatenate([cotangent, jnp.zeros((1, width), cotangent.dtype)], axis=0)
    padded_g = jnp.concatenate([gates.reshape(-1), jnp.zeros((1,), gates.dtype)], axis=0)
    send_g = padded_g[source]
    g_cols = jnp.where(
        jnp.arange(LANE, dtype=jnp.int32)[None, :] == 0, send_g[:, None], jnp.zeros((), gates.dtype)
    )
    packed = jnp.concatenate([padded_x[token_index], padded_dy[token_index], g_cols], axis=1)
    row_width = packed.shape[1]
    packed = packed.reshape(axis_len, CAP, row_width)
    recv = lax.all_to_all(packed, "expert", split_axis=0, concat_axis=0, tiled=True)
    w_gate = gate_w[0]
    w_up = up_w[0]
    w_down = down_w[0]
    other_gate, other_up, other_down = partner((gate_w, up_w, down_w), "expert", pair_bit)
    taken = own_flag == 1
    w_gate = jnp.where(taken, other_gate[0], w_gate)
    w_up = jnp.where(taken, other_up[0], w_up)
    w_down = jnp.where(taken, other_down[0], w_down)
    gathered = dp_gather(recv)
    block_count = lax.axis_size("dp")
    row_x = gathered[:, :, :width]
    row_dy = gathered[:, :, width:2 * width]
    row_g = gathered[:, :, 2 * width:2 * width + 1]
    feature = (((2,), (0,)), ((), ()))
    rows_contract = (((0, 1), (0, 1)), ((), ()))
    pre_gate = lax.dot_general(row_x, w_gate, feature, preferred_element_type=jnp.float32)
    pre_up = lax.dot_general(row_x, w_up, feature, preferred_element_type=jnp.float32)
    sigma = jax.nn.sigmoid(pre_gate)
    active = pre_gate * sigma
    hidden = (active * pre_up).astype(jnp.bfloat16)
    back = lax.dot_general(
        row_dy, w_down, (((2,), (1,)), ((), ())), preferred_element_type=jnp.float32
    )
    score = jnp.sum(hidden.astype(jnp.float32) * back, axis=2)
    scaled = row_dy * row_g
    d_hidden = row_g.astype(jnp.float32) * back
    d_gate = (d_hidden * pre_up * sigma * (1.0 + pre_gate * (1.0 - sigma))).astype(jnp.bfloat16)
    d_up = (d_hidden * active).astype(jnp.bfloat16)
    grad_gate = lax.dot_general(row_x, d_gate, rows_contract, preferred_element_type=jnp.float32)
    grad_up = lax.dot_general(row_x, d_up, rows_contract, preferred_element_type=jnp.float32)
    grad_down = lax.dot_general(hidden, scaled, rows_contract, preferred_element_type=jnp.float32)
    scores = score.reshape(block_count, axis_len * CAP)
    parts = lax.all_to_all(scores, "dp", split_axis=0, concat_axis=0, tiled=True)
    own_scores = jnp.sum(parts, axis=0).reshape(axis_len, CAP)
    returned = lax.all_to_all(own_scores, "expert", split_axis=0, concat_axis=0, tiled=True)
    picked = returned.reshape(-1)[jnp.minimum(slots, slot_count - 1)]
    score_grad = jnp.where(valid, picked, 0.0).reshape(tok_count, top_count)
    out_gate = grad_gate.astype(jnp.bfloat16)[None]
    out_up = grad_up.astype(jnp.bfloat16)[None]
    out_down = grad_down.astype(jnp.bfloat16)[None]
    return (out_gate, out_up, out_down, score_grad)


def solution(mesh):
    placed = (
        P(("dp", "expert"), None),
        P(("dp", "expert"), None),
        P(("dp", "expert"), None),
        P(("dp", "expert"), None),
        P(),
        P("expert", None, "dp"),
        P("expert", None, "dp"),
        P("expert", "dp", None),
    )
    return jax.shard_map(
        body,
        mesh=mesh,
        in_specs=placed,
        out_specs=(
            P("expert", None, "dp"),
            P("expert", None, "dp"),
            P("expert", "dp", None),
            P(("dp", "expert"), None),
        ),
        check_vma=False,
    )
```

```python
import functools

import jax
import jax.numpy as jnp
from jax import lax
from jax.experimental import pallas as pl
from jax.experimental.pallas import tpu as pltpu
from jax.sharding import PartitionSpec as P

CAP = 6
LANE = 128


def partner(block, axis, stride):
    count = lax.axis_size(axis)
    route = []
    for low in range(count):
        high = low | 1 << stride
        if high != low and high < count:
            route += [(low, high), (high, low)]
    return lax.ppermute(block, axis, route)


def dp_gather_kernel(n_dp, ring, chunks, x_ref, o_ref, recv, recv_z, send):
    me = lax.axis_index("dp")
    ex = lax.axis_index("expert")
    rows = x_ref.shape[1]
    half = rows // 2
    piece = rows // chunks
    plane = me // ring
    pos = me % ring
    left = plane * ring + (pos + ring - 1) % ring
    right = plane * ring + (pos + 1) % ring
    far = plane * ring + (pos + 2) % ring
    across = (me + ring) % n_dp

    def span(k, start, size):
        return o_ref.at[:, pl.ds(k * rows + start, size), :]

    def push(src, dst, slot, sem, peer):
        copy = pltpu.make_async_remote_copy(
            src_ref=src,
            dst_ref=dst,
            send_sem=send.at[slot],
            recv_sem=sem,
            device_id=(peer, ex),
            device_id_type=pl.DeviceIdType.MESH,
        )
        copy.start()
        return copy

    def arrived(ref, sem):
        pltpu.make_async_copy(ref, ref, sem).wait()

    barrier = pltpu.get_barrier_semaphore()
    for peer in (left, right, across):
        pl.semaphore_signal(barrier, inc=1, device_id=(peer, ex), device_id_type=pl.DeviceIdType.MESH)
    pl.semaphore_wait(barrier, 3)

    local = pltpu.make_async_copy(x_ref, span(me, 0, rows), recv.at[me])
    local.start()
    sent = []
    for q in range(chunks):
        sent.append(
            push(
                x_ref.at[:, pl.ds(q * piece, piece), :],
                span(me, q * piece, piece),
                len(sent),
                recv_z.at[q],
                across,
            )
        )
    sent.append(push(x_ref, span(me, 0, rows), len(sent), recv.at[me], left))
    sent.append(push(x_ref, span(me, 0, rows), len(sent), recv.at[me], right))
    arrived(span(left, 0, rows), recv.at[left])
    sent.append(push(span(left, 0, half), span(left, 0, half), len(sent), recv.at[left], right))
    arrived(span(right, 0, rows), recv.at[right])
    sent.append(push(span(right, half, half), span(right, half, half), len(sent), recv.at[right], left))
    for q in range(chunks):
        chunk = span(across, q * piece, piece)
        arrived(chunk, recv_z.at[q])
        sent.append(push(chunk, chunk, len(sent), recv.at[across], left))
        sent.append(push(chunk, chunk, len(sent), recv.at[across], right))
    left_across = (left + ring) % n_dp
    right_across = (right + ring) % n_dp
    arrived(span(left_across, 0, rows), recv.at[left_across])
    sent.append(
        push(span(left_across, 0, half), span(left_across, 0, half), len(sent), recv.at[left_across], right)
    )
    arrived(span(right_across, 0, rows), recv.at[right_across])
    sent.append(
        push(span(right_across, half, half), span(right_across, half, half), len(sent), recv.at[right_across], left)
    )
    arrived(span(far, 0, rows), recv.at[far])
    far_across = (far + ring) % n_dp
    arrived(span(far_across, 0, rows), recv.at[far_across])
    local.wait()
    for copy in sent:
        copy.wait_send()


def dp_gather(block):
    n_dp = lax.axis_size("dp")
    ring = n_dp // 2
    chunks = 4
    cap, rows, row_width = block.shape
    sends = 3 * chunks + 6
    return pl.pallas_call(
        functools.partial(dp_gather_kernel, n_dp, ring, chunks),
        out_shape=jax.ShapeDtypeStruct((cap, n_dp * rows, row_width), block.dtype),
        in_specs=[pl.BlockSpec(memory_space=pl.ANY)],
        out_specs=pl.BlockSpec(memory_space=pl.ANY),
        scratch_shapes=[
            pltpu.SemaphoreType.DMA((n_dp,)),
            pltpu.SemaphoreType.DMA((chunks,)),
            pltpu.SemaphoreType.DMA((sends,)),
        ],
        compiler_params=pltpu.CompilerParams(collective_id=0, has_side_effects=True),
    )(block)


def expert_exchange_kernel(n_ex, x_ref, o_ref, recv, send, local_sem):
    me = lax.axis_index("expert")
    dp = lax.axis_index("dp")
    barrier = pltpu.get_barrier_semaphore()
    for step in range(1, n_ex):
        peer = (me + step) % n_ex
        pl.semaphore_signal(barrier, inc=1, device_id=(dp, peer), device_id_type=pl.DeviceIdType.MESH)
    pl.semaphore_wait(barrier, n_ex - 1)
    local = pltpu.make_async_copy(x_ref.at[pl.ds(me, 1)], o_ref.at[pl.ds(me, 1)], local_sem.at[0])
    local.start()
    sent = []
    for step in range(1, n_ex):
        peer = (me + step) % n_ex
        copy = pltpu.make_async_remote_copy(
            src_ref=x_ref.at[pl.ds(peer, 1)],
            dst_ref=o_ref.at[pl.ds(me, 1)],
            send_sem=send.at[step],
            recv_sem=recv.at[0],
            device_id=(dp, peer),
            device_id_type=pl.DeviceIdType.MESH,
        )
        copy.start()
        sent.append(copy)
    pltpu.make_async_copy(
        x_ref.at[pl.ds(0, n_ex - 1)], o_ref.at[pl.ds(0, n_ex - 1)], recv.at[0]
    ).wait()
    local.wait()
    for copy in sent:
        copy.wait_send()


def expert_exchange(block):
    n_ex = lax.axis_size("expert")
    return pl.pallas_call(
        functools.partial(expert_exchange_kernel, n_ex),
        out_shape=jax.ShapeDtypeStruct(block.shape, block.dtype),
        in_specs=[pl.BlockSpec(memory_space=pl.ANY)],
        out_specs=pl.BlockSpec(memory_space=pl.ANY),
        scratch_shapes=[
            pltpu.SemaphoreType.DMA((1,)),
            pltpu.SemaphoreType.DMA((n_ex,)),
            pltpu.SemaphoreType.DMA((1,)),
        ],
        compiler_params=pltpu.CompilerParams(collective_id=1, has_side_effects=True),
    )(block)


def body(tokens, cotangent, expert_ids, gates, swap_flags, gate_w, up_w, down_w):
    axis_len = lax.axis_size("expert")
    half_axis = axis_len // 2
    pair_bit = axis_len.bit_length() - 2
    own_slot = lax.axis_index("expert")
    tok_count = tokens.shape[0]
    top_count = expert_ids.shape[1]
    width = tokens.shape[1]
    flat_ids = expert_ids.reshape(-1)
    choice_count = flat_ids.shape[0]
    valid = flat_ids < axis_len
    pair_index = jnp.arange(half_axis, dtype=jnp.int32)
    flag_of = jnp.sum(
        jnp.where((flat_ids % half_axis)[:, None] == pair_index[None, :], swap_flags[None, :], 0),
        axis=1,
    )
    own_flag = jnp.sum(jnp.where(pair_index == own_slot % half_axis, swap_flags, 0))
    target = jnp.where(flag_of == 1, jnp.bitwise_xor(flat_ids, half_axis), flat_ids)
    target = jnp.where(valid, target, 0)
    onehot = jnp.where(
        (target[:, None] == jnp.arange(axis_len, dtype=jnp.int32)[None, :]) & valid[:, None], 1, 0
    ).astype(jnp.int32)
    ranks = jnp.sum(jnp.cumsum(onehot, axis=0) * onehot, axis=1) - 1
    slot_count = axis_len * CAP
    slots = jnp.where(valid, target * CAP + ranks, slot_count)
    source = (
        jnp.full((slot_count,), choice_count, jnp.int32)
        .at[slots]
        .set(jnp.arange(choice_count, dtype=jnp.int32), mode="drop")
    )
    token_index = source // top_count
    padded_x = jnp.concatenate([tokens, jnp.zeros((1, width), tokens.dtype)], axis=0)
    padded_dy = jnp.concatenate([cotangent, jnp.zeros((1, width), cotangent.dtype)], axis=0)
    padded_g = jnp.concatenate([gates.reshape(-1), jnp.zeros((1,), gates.dtype)], axis=0)
    send_g = padded_g[source]
    g_cols = jnp.where(
        jnp.arange(LANE, dtype=jnp.int32)[None, :] == 0, send_g[:, None], jnp.zeros((), gates.dtype)
    )
    packed = jnp.concatenate([padded_x[token_index], padded_dy[token_index], g_cols], axis=1)
    row_width = packed.shape[1]
    packed = packed.reshape(axis_len, CAP * row_width // LANE, LANE)
    recv = expert_exchange(packed).reshape(axis_len, CAP, row_width)
    recv = jnp.transpose(recv, (1, 0, 2))
    w_gate = gate_w[0]
    w_up = up_w[0]
    w_down = down_w[0]
    other_gate, other_up, other_down = partner((gate_w, up_w, down_w), "expert", pair_bit)
    taken = own_flag == 1
    w_gate = jnp.where(taken, other_gate[0], w_gate)
    w_up = jnp.where(taken, other_up[0], w_up)
    w_down = jnp.where(taken, other_down[0], w_down)
    gathered = dp_gather(recv)
    block_count = lax.axis_size("dp")
    row_x = gathered[:, :, :width]
    row_dy = gathered[:, :, width:2 * width]
    row_g = gathered[:, :, 2 * width:2 * width + 1]
    feature = (((2,), (0,)), ((), ()))
    rows_contract = (((0, 1), (0, 1)), ((), ()))
    pre_gate = lax.dot_general(row_x, w_gate, feature, preferred_element_type=jnp.float32)
    pre_up = lax.dot_general(row_x, w_up, feature, preferred_element_type=jnp.float32)
    sigma = jax.nn.sigmoid(pre_gate)
    active = pre_gate * sigma
    hidden = (active * pre_up).astype(jnp.bfloat16)
    back = lax.dot_general(
        row_dy, w_down, (((2,), (1,)), ((), ())), preferred_element_type=jnp.float32
    )
    score = jnp.sum(hidden.astype(jnp.float32) * back, axis=2).T
    scaled = row_dy * row_g
    d_hidden = row_g.astype(jnp.float32) * back
    d_gate = (d_hidden * pre_up * sigma * (1.0 + pre_gate * (1.0 - sigma))).astype(jnp.bfloat16)
    d_up = (d_hidden * active).astype(jnp.bfloat16)
    grad_gate = lax.dot_general(row_x, d_gate, rows_contract, preferred_element_type=jnp.float32)
    grad_up = lax.dot_general(row_x, d_up, rows_contract, preferred_element_type=jnp.float32)
    grad_down = lax.dot_general(hidden, scaled, rows_contract, preferred_element_type=jnp.float32)
    scores = score.reshape(block_count, axis_len * CAP)
    parts = lax.all_to_all(scores, "dp", split_axis=0, concat_axis=0, tiled=True)
    own_scores = jnp.sum(parts, axis=0).reshape(axis_len, CAP)
    returned = lax.all_to_all(own_scores, "expert", split_axis=0, concat_axis=0, tiled=True)
    picked = returned.reshape(-1)[jnp.minimum(slots, slot_count - 1)]
    score_grad = jnp.where(valid, picked, 0.0).reshape(tok_count, top_count)
    out_gate = grad_gate.astype(jnp.bfloat16)[None]
    out_up = grad_up.astype(jnp.bfloat16)[None]
    out_down = grad_down.astype(jnp.bfloat16)[None]
    return (out_gate, out_up, out_down, score_grad)


def solution(mesh):
    placed = (
        P(("dp", "expert"), None),
        P(("dp", "expert"), None),
        P(("dp", "expert"), None),
        P(("dp", "expert"), None),
        P(),
        P("expert", None, "dp"),
        P("expert", None, "dp"),
        P("expert", "dp", None),
    )
    return jax.shard_map(
        body,
        mesh=mesh,
        in_specs=placed,
        out_specs=(
            P("expert", None, "dp"),
            P("expert", None, "dp"),
            P("expert", "dp", None),
            P(("dp", "expert"), None),
        ),
        check_vma=False,
    )
```

```python
import functools

import jax
import jax.numpy as jnp
from jax import lax
from jax.experimental import pallas as pl
from jax.experimental.pallas import tpu as pltpu
from jax.sharding import PartitionSpec as P

CAP = 6
LANE = 128


def dp_gather_kernel(n_dp, ring, chunks, n_ex, x_ref, wg_ref, wu_ref, wd_ref, o_ref, og_ref, ou_ref, od_ref, recv, recv_z, recv_w, send):
    me = lax.axis_index("dp")
    ex = lax.axis_index("expert")
    rows = x_ref.shape[1]
    half = rows // 2
    piece = rows // chunks
    plane = me // ring
    pos = me % ring
    left = plane * ring + (pos + ring - 1) % ring
    right = plane * ring + (pos + 1) % ring
    far = plane * ring + (pos + 2) % ring
    across = (me + ring) % n_dp
    twin = (ex + n_ex // 2) % n_ex

    def span(k, start, size):
        return o_ref.at[:, pl.ds(k * rows + start, size), :]

    def push(src, dst, slot, sem, peer):
        copy = pltpu.make_async_remote_copy(
            src_ref=src,
            dst_ref=dst,
            send_sem=send.at[slot],
            recv_sem=sem,
            device_id=(peer, ex),
            device_id_type=pl.DeviceIdType.MESH,
        )
        copy.start()
        return copy

    def arrived(ref, sem):
        pltpu.make_async_copy(ref, ref, sem).wait()

    barrier = pltpu.get_barrier_semaphore()
    for peer in (left, right, across):
        pl.semaphore_signal(barrier, inc=1, device_id=(peer, ex), device_id_type=pl.DeviceIdType.MESH)
    pl.semaphore_signal(barrier, inc=1, device_id=(me, twin), device_id_type=pl.DeviceIdType.MESH)
    pl.semaphore_wait(barrier, 4)

    local = pltpu.make_async_copy(x_ref, span(me, 0, rows), recv.at[me])
    local.start()
    swaps = []
    for index, (src, dst) in enumerate(((wg_ref, og_ref), (wu_ref, ou_ref), (wd_ref, od_ref))):
        copy = pltpu.make_async_remote_copy(
            src_ref=src,
            dst_ref=dst,
            send_sem=send.at[3 * chunks + 6 + index],
            recv_sem=recv_w.at[index],
            device_id=(me, twin),
            device_id_type=pl.DeviceIdType.MESH,
        )
        copy.start()
        swaps.append(copy)
    sent = []
    for q in range(chunks):
        sent.append(
            push(
                x_ref.at[:, pl.ds(q * piece, piece), :],
                span(me, q * piece, piece),
                len(sent),
                recv_z.at[q],
                across,
            )
        )
    sent.append(push(x_ref, span(me, 0, rows), len(sent), recv.at[me], left))
    sent.append(push(x_ref, span(me, 0, rows), len(sent), recv.at[me], right))
    arrived(span(left, 0, rows), recv.at[left])
    sent.append(push(span(left, 0, half), span(left, 0, half), len(sent), recv.at[left], right))
    arrived(span(right, 0, rows), recv.at[right])
    sent.append(push(span(right, half, half), span(right, half, half), len(sent), recv.at[right], left))
    for q in range(chunks):
        chunk = span(across, q * piece, piece)
        arrived(chunk, recv_z.at[q])
        sent.append(push(chunk, chunk, len(sent), recv.at[across], left))
        sent.append(push(chunk, chunk, len(sent), recv.at[across], right))
    left_across = (left + ring) % n_dp
    right_across = (right + ring) % n_dp
    arrived(span(left_across, 0, rows), recv.at[left_across])
    sent.append(
        push(span(left_across, 0, half), span(left_across, 0, half), len(sent), recv.at[left_across], right)
    )
    arrived(span(right_across, 0, rows), recv.at[right_across])
    sent.append(
        push(span(right_across, half, half), span(right_across, half, half), len(sent), recv.at[right_across], left)
    )
    arrived(span(far, 0, rows), recv.at[far])
    far_across = (far + ring) % n_dp
    arrived(span(far_across, 0, rows), recv.at[far_across])
    local.wait()
    for copy in sent:
        copy.wait_send()
    for copy in swaps:
        copy.wait()


def dp_gather(block, w_gate, w_up, w_down):
    n_dp = lax.axis_size("dp")
    n_ex = lax.axis_size("expert")
    ring = n_dp // 2
    chunks = 4
    cap, rows, row_width = block.shape
    sends = 3 * chunks + 6 + 3
    weights = (w_gate, w_up, w_down)
    return pl.pallas_call(
        functools.partial(dp_gather_kernel, n_dp, ring, chunks, n_ex),
        out_shape=(jax.ShapeDtypeStruct((cap, n_dp * rows, row_width), block.dtype),)
        + tuple(jax.ShapeDtypeStruct(w.shape, w.dtype) for w in weights),
        in_specs=[pl.BlockSpec(memory_space=pl.ANY)] * 4,
        out_specs=(pl.BlockSpec(memory_space=pl.ANY),) * 4,
        scratch_shapes=[
            pltpu.SemaphoreType.DMA((n_dp,)),
            pltpu.SemaphoreType.DMA((chunks,)),
            pltpu.SemaphoreType.DMA((3,)),
            pltpu.SemaphoreType.DMA((sends,)),
        ],
        compiler_params=pltpu.CompilerParams(collective_id=0, has_side_effects=True),
    )(block, w_gate, w_up, w_down)


def expert_exchange_kernel(n_ex, x_ref, o_ref, recv, send, local_sem):
    me = lax.axis_index("expert")
    dp = lax.axis_index("dp")
    barrier = pltpu.get_barrier_semaphore()
    for step in range(1, n_ex):
        peer = (me + step) % n_ex
        pl.semaphore_signal(barrier, inc=1, device_id=(dp, peer), device_id_type=pl.DeviceIdType.MESH)
    pl.semaphore_wait(barrier, n_ex - 1)
    local = pltpu.make_async_copy(x_ref.at[pl.ds(me, 1)], o_ref.at[pl.ds(me, 1)], local_sem.at[0])
    local.start()
    sent = []
    for step in range(1, n_ex):
        peer = (me + step) % n_ex
        copy = pltpu.make_async_remote_copy(
            src_ref=x_ref.at[pl.ds(peer, 1)],
            dst_ref=o_ref.at[pl.ds(me, 1)],
            send_sem=send.at[step],
            recv_sem=recv.at[0],
            device_id=(dp, peer),
            device_id_type=pl.DeviceIdType.MESH,
        )
        copy.start()
        sent.append(copy)
    pltpu.make_async_copy(
        x_ref.at[pl.ds(0, n_ex - 1)], o_ref.at[pl.ds(0, n_ex - 1)], recv.at[0]
    ).wait()
    local.wait()
    for copy in sent:
        copy.wait_send()


def expert_exchange(block):
    n_ex = lax.axis_size("expert")
    return pl.pallas_call(
        functools.partial(expert_exchange_kernel, n_ex),
        out_shape=jax.ShapeDtypeStruct(block.shape, block.dtype),
        in_specs=[pl.BlockSpec(memory_space=pl.ANY)],
        out_specs=pl.BlockSpec(memory_space=pl.ANY),
        scratch_shapes=[
            pltpu.SemaphoreType.DMA((1,)),
            pltpu.SemaphoreType.DMA((n_ex,)),
            pltpu.SemaphoreType.DMA((1,)),
        ],
        compiler_params=pltpu.CompilerParams(collective_id=1, has_side_effects=True),
    )(block)


def body(tokens, cotangent, expert_ids, gates, swap_flags, gate_w, up_w, down_w):
    axis_len = lax.axis_size("expert")
    half_axis = axis_len // 2
    own_slot = lax.axis_index("expert")
    tok_count = tokens.shape[0]
    top_count = expert_ids.shape[1]
    width = tokens.shape[1]
    flat_ids = expert_ids.reshape(-1)
    choice_count = flat_ids.shape[0]
    valid = flat_ids < axis_len
    pair_index = jnp.arange(half_axis, dtype=jnp.int32)
    flag_of = jnp.sum(
        jnp.where((flat_ids % half_axis)[:, None] == pair_index[None, :], swap_flags[None, :], 0),
        axis=1,
    )
    own_flag = jnp.sum(jnp.where(pair_index == own_slot % half_axis, swap_flags, 0))
    target = jnp.where(flag_of == 1, jnp.bitwise_xor(flat_ids, half_axis), flat_ids)
    target = jnp.where(valid, target, 0)
    onehot = (
        (target[:, None] == jnp.arange(axis_len, dtype=jnp.int32)[None, :]) & valid[:, None]
    ).astype(jnp.bfloat16)
    order = jnp.arange(choice_count, dtype=jnp.int32)
    lower = (order[None, :] <= order[:, None]).astype(jnp.bfloat16)
    counts = jnp.dot(lower, onehot, preferred_element_type=jnp.float32)
    ranks = jnp.sum(counts * onehot.astype(jnp.float32), axis=1).astype(jnp.int32) - 1
    slot_count = axis_len * CAP
    slots = jnp.where(valid, target * CAP + ranks, slot_count)
    pick = (slots[:, None] == jnp.arange(slot_count, dtype=jnp.int32)[None, :]).astype(jnp.bfloat16)
    token_pick = jnp.sum(pick.reshape(tok_count, top_count, slot_count).astype(jnp.float32), axis=1)
    token_pick = token_pick.astype(jnp.bfloat16)
    rows_xdy = lax.dot_general(
        token_pick,
        jnp.concatenate([tokens, cotangent], axis=1),
        (((0,), (0,)), ((), ())),
        preferred_element_type=jnp.float32,
    ).astype(tokens.dtype)
    send_g = jnp.dot(gates.reshape(1, -1), pick, preferred_element_type=jnp.float32).astype(gates.dtype)
    g_cols = jnp.where(
        jnp.arange(LANE, dtype=jnp.int32)[None, :] == 0, send_g.reshape(-1, 1), jnp.zeros((), gates.dtype)
    )
    packed = jnp.concatenate([rows_xdy, g_cols], axis=1)
    row_width = packed.shape[1]
    packed = packed.reshape(axis_len, CAP * row_width // LANE, LANE)
    recv = expert_exchange(packed).reshape(axis_len, CAP, row_width)
    recv = jnp.transpose(recv, (1, 0, 2))
    gathered, other_gate, other_up, other_down = dp_gather(recv, gate_w, up_w, down_w)
    taken = own_flag == 1
    w_gate = jnp.where(taken, other_gate[0], gate_w[0])
    w_up = jnp.where(taken, other_up[0], up_w[0])
    w_down = jnp.where(taken, other_down[0], down_w[0])
    block_count = lax.axis_size("dp")
    row_x = gathered[:, :, :width]
    row_dy = gathered[:, :, width:2 * width]
    row_g = gathered[:, :, 2 * width:2 * width + 1]
    feature = (((2,), (0,)), ((), ()))
    rows_contract = (((0, 1), (0, 1)), ((), ()))
    hidden_count = w_gate.shape[1]
    w_both = jnp.concatenate([w_gate, w_up], axis=1)
    pre_both = lax.dot_general(row_x, w_both, feature, preferred_element_type=jnp.float32)
    pre_gate = pre_both[:, :, :hidden_count]
    pre_up = pre_both[:, :, hidden_count:]
    sigma = jax.nn.sigmoid(pre_gate)
    active = pre_gate * sigma
    hidden = (active * pre_up).astype(jnp.bfloat16)
    back = lax.dot_general(
        row_dy, w_down, (((2,), (1,)), ((), ())), preferred_element_type=jnp.float32
    )
    score = jnp.sum(hidden.astype(jnp.float32) * back, axis=2).T
    scaled = row_dy * row_g
    d_hidden = row_g.astype(jnp.float32) * back
    d_gate = (d_hidden * pre_up * sigma * (1.0 + pre_gate * (1.0 - sigma))).astype(jnp.bfloat16)
    d_up = (d_hidden * active).astype(jnp.bfloat16)
    d_both = jnp.concatenate([d_gate, d_up], axis=2)
    grad_both = lax.dot_general(row_x, d_both, rows_contract, preferred_element_type=jnp.float32)
    grad_gate = grad_both[:, :hidden_count]
    grad_up = grad_both[:, hidden_count:]
    grad_down = lax.dot_general(hidden, scaled, rows_contract, preferred_element_type=jnp.float32)
    scores = score.reshape(block_count, axis_len * CAP)
    parts = lax.all_to_all(scores, "dp", split_axis=0, concat_axis=0, tiled=True)
    own_scores = jnp.sum(parts, axis=0).reshape(axis_len, CAP)
    returned = lax.all_to_all(own_scores, "expert", split_axis=0, concat_axis=0, tiled=True)
    picked = jnp.sum(jnp.where(pick > 0, returned.reshape(1, -1), 0.0), axis=1)
    score_grad = jnp.where(valid, picked, 0.0).reshape(tok_count, top_count)
    out_gate = grad_gate.astype(jnp.bfloat16)[None]
    out_up = grad_up.astype(jnp.bfloat16)[None]
    out_down = grad_down.astype(jnp.bfloat16)[None]
    return (out_gate, out_up, out_down, score_grad)


def solution(mesh):
    placed = (
        P(("dp", "expert"), None),
        P(("dp", "expert"), None),
        P(("dp", "expert"), None),
        P(("dp", "expert"), None),
        P(),
        P("expert", None, "dp"),
        P("expert", None, "dp"),
        P("expert", "dp", None),
    )
    return jax.shard_map(
        body,
        mesh=mesh,
        in_specs=placed,
        out_specs=(
            P("expert", None, "dp"),
            P("expert", None, "dp"),
            P("expert", "dp", None),
            P(("dp", "expert"), None),
        ),
        check_vma=False,
    )
```

```python
import functools

import jax
import jax.numpy as jnp
from jax import lax
from jax.experimental import pallas as pl
from jax.experimental.pallas import tpu as pltpu
from jax.sharding import PartitionSpec as P

CAP = 6
LANE = 128


def dp_gather_kernel(n_dp, ring, chunks, n_ex, x_ref, wg_ref, wu_ref, wd_ref, o_ref, og_ref, ou_ref, od_ref, recv, recv_z, recv_w, send):
    me = lax.axis_index("dp")
    ex = lax.axis_index("expert")
    rows = x_ref.shape[1]
    half = rows // 2
    piece = rows // chunks
    plane = me // ring
    pos = me % ring
    left = plane * ring + (pos + ring - 1) % ring
    right = plane * ring + (pos + 1) % ring
    far = plane * ring + (pos + 2) % ring
    across = (me + ring) % n_dp
    twin = (ex + n_ex // 2) % n_ex

    def span(k, start, size):
        return o_ref.at[:, pl.ds(k * rows + start, size), :]

    def push(src, dst, slot, sem, peer):
        copy = pltpu.make_async_remote_copy(
            src_ref=src,
            dst_ref=dst,
            send_sem=send.at[slot],
            recv_sem=sem,
            device_id=(peer, ex),
            device_id_type=pl.DeviceIdType.MESH,
        )
        copy.start()
        return copy

    def arrived(ref, sem):
        pltpu.make_async_copy(ref, ref, sem).wait()

    barrier = pltpu.get_barrier_semaphore()
    for peer in (left, right, across):
        pl.semaphore_signal(barrier, inc=1, device_id=(peer, ex), device_id_type=pl.DeviceIdType.MESH)
    pl.semaphore_signal(barrier, inc=1, device_id=(me, twin), device_id_type=pl.DeviceIdType.MESH)
    pl.semaphore_wait(barrier, 4)

    local = pltpu.make_async_copy(x_ref, span(me, 0, rows), recv.at[me])
    local.start()
    sent = []
    for q in range(chunks):
        sent.append(
            push(
                x_ref.at[:, pl.ds(q * piece, piece), :],
                span(me, q * piece, piece),
                len(sent),
                recv_z.at[q],
                across,
            )
        )
    sent.append(push(x_ref, span(me, 0, rows), len(sent), recv.at[me], left))
    sent.append(push(x_ref, span(me, 0, rows), len(sent), recv.at[me], right))
    arrived(span(left, 0, rows), recv.at[left])
    sent.append(push(span(left, 0, half), span(left, 0, half), len(sent), recv.at[left], right))
    arrived(span(right, 0, rows), recv.at[right])
    sent.append(push(span(right, half, half), span(right, half, half), len(sent), recv.at[right], left))
    for q in range(chunks):
        chunk = span(across, q * piece, piece)
        arrived(chunk, recv_z.at[q])
        sent.append(push(chunk, chunk, len(sent), recv.at[across], left))
        sent.append(push(chunk, chunk, len(sent), recv.at[across], right))
    swaps = []
    for index, (src, dst) in enumerate(((wg_ref, og_ref), (wu_ref, ou_ref), (wd_ref, od_ref))):
        copy = pltpu.make_async_remote_copy(
            src_ref=src,
            dst_ref=dst,
            send_sem=send.at[3 * chunks + 6 + index],
            recv_sem=recv_w.at[index],
            device_id=(me, twin),
            device_id_type=pl.DeviceIdType.MESH,
        )
        copy.start()
        swaps.append(copy)
    left_across = (left + ring) % n_dp
    right_across = (right + ring) % n_dp
    arrived(span(left_across, 0, rows), recv.at[left_across])
    sent.append(
        push(span(left_across, 0, half), span(left_across, 0, half), len(sent), recv.at[left_across], right)
    )
    arrived(span(right_across, 0, rows), recv.at[right_across])
    sent.append(
        push(span(right_across, half, half), span(right_across, half, half), len(sent), recv.at[right_across], left)
    )
    arrived(span(far, 0, rows), recv.at[far])
    far_across = (far + ring) % n_dp
    arrived(span(far_across, 0, rows), recv.at[far_across])
    local.wait()
    for copy in sent:
        copy.wait_send()
    for copy in swaps:
        copy.wait()


def dp_gather(block, w_gate, w_up, w_down):
    n_dp = lax.axis_size("dp")
    n_ex = lax.axis_size("expert")
    ring = n_dp // 2
    chunks = 4
    cap, rows, row_width = block.shape
    sends = 3 * chunks + 6 + 3
    weights = (w_gate, w_up, w_down)
    return pl.pallas_call(
        functools.partial(dp_gather_kernel, n_dp, ring, chunks, n_ex),
        out_shape=(jax.ShapeDtypeStruct((cap, n_dp * rows, row_width), block.dtype),)
        + tuple(jax.ShapeDtypeStruct(w.shape, w.dtype) for w in weights),
        in_specs=[pl.BlockSpec(memory_space=pl.ANY)] * 4,
        out_specs=(pl.BlockSpec(memory_space=pl.ANY),) * 4,
        scratch_shapes=[
            pltpu.SemaphoreType.DMA((n_dp,)),
            pltpu.SemaphoreType.DMA((chunks,)),
            pltpu.SemaphoreType.DMA((3,)),
            pltpu.SemaphoreType.DMA((sends,)),
        ],
        compiler_params=pltpu.CompilerParams(collective_id=0, has_side_effects=True),
    )(block, w_gate, w_up, w_down)


def expert_exchange_kernel(n_ex, x_ref, o_ref, recv, send, local_sem):
    me = lax.axis_index("expert")
    dp = lax.axis_index("dp")
    barrier = pltpu.get_barrier_semaphore()
    for step in range(1, n_ex):
        peer = (me + step) % n_ex
        pl.semaphore_signal(barrier, inc=1, device_id=(dp, peer), device_id_type=pl.DeviceIdType.MESH)
    pl.semaphore_wait(barrier, n_ex - 1)
    local = pltpu.make_async_copy(x_ref.at[pl.ds(me, 1)], o_ref.at[pl.ds(me, 1)], local_sem.at[0])
    local.start()
    sent = []
    for step in range(1, n_ex):
        peer = (me + step) % n_ex
        copy = pltpu.make_async_remote_copy(
            src_ref=x_ref.at[pl.ds(peer, 1)],
            dst_ref=o_ref.at[pl.ds(me, 1)],
            send_sem=send.at[step],
            recv_sem=recv.at[0],
            device_id=(dp, peer),
            device_id_type=pl.DeviceIdType.MESH,
        )
        copy.start()
        sent.append(copy)
    pltpu.make_async_copy(
        x_ref.at[pl.ds(0, n_ex - 1)], o_ref.at[pl.ds(0, n_ex - 1)], recv.at[0]
    ).wait()
    local.wait()
    for copy in sent:
        copy.wait_send()


def expert_exchange(block):
    n_ex = lax.axis_size("expert")
    return pl.pallas_call(
        functools.partial(expert_exchange_kernel, n_ex),
        out_shape=jax.ShapeDtypeStruct(block.shape, block.dtype),
        in_specs=[pl.BlockSpec(memory_space=pl.ANY)],
        out_specs=pl.BlockSpec(memory_space=pl.ANY),
        scratch_shapes=[
            pltpu.SemaphoreType.DMA((1,)),
            pltpu.SemaphoreType.DMA((n_ex,)),
            pltpu.SemaphoreType.DMA((1,)),
        ],
        compiler_params=pltpu.CompilerParams(collective_id=1, has_side_effects=True),
    )(block)


def body(tokens, cotangent, expert_ids, gates, swap_flags, gate_w, up_w, down_w):
    axis_len = lax.axis_size("expert")
    half_axis = axis_len // 2
    own_slot = lax.axis_index("expert")
    tok_count = tokens.shape[0]
    top_count = expert_ids.shape[1]
    width = tokens.shape[1]
    flat_ids = expert_ids.reshape(-1)
    choice_count = flat_ids.shape[0]
    valid = flat_ids < axis_len
    pair_index = jnp.arange(half_axis, dtype=jnp.int32)
    flag_of = jnp.sum(
        jnp.where((flat_ids % half_axis)[:, None] == pair_index[None, :], swap_flags[None, :], 0),
        axis=1,
    )
    own_flag = jnp.sum(jnp.where(pair_index == own_slot % half_axis, swap_flags, 0))
    target = jnp.where(flag_of == 1, jnp.bitwise_xor(flat_ids, half_axis), flat_ids)
    target = jnp.where(valid, target, 0)
    onehot = (
        (target[:, None] == jnp.arange(axis_len, dtype=jnp.int32)[None, :]) & valid[:, None]
    ).astype(jnp.bfloat16)
    order = jnp.arange(choice_count, dtype=jnp.int32)
    lower = (order[None, :] <= order[:, None]).astype(jnp.bfloat16)
    counts = jnp.dot(lower, onehot, preferred_element_type=jnp.float32)
    ranks = jnp.sum(counts * onehot.astype(jnp.float32), axis=1).astype(jnp.int32) - 1
    slot_count = axis_len * CAP
    slots = jnp.where(valid, target * CAP + ranks, slot_count)
    pick = (slots[:, None] == jnp.arange(slot_count, dtype=jnp.int32)[None, :]).astype(jnp.bfloat16)
    token_pick = jnp.sum(pick.reshape(tok_count, top_count, slot_count).astype(jnp.float32), axis=1)
    token_pick = token_pick.astype(jnp.bfloat16)
    rows_xdy = lax.dot_general(
        token_pick,
        jnp.concatenate([tokens, cotangent], axis=1),
        (((0,), (0,)), ((), ())),
        preferred_element_type=jnp.float32,
    ).astype(tokens.dtype)
    send_g = jnp.dot(gates.reshape(1, -1), pick, preferred_element_type=jnp.float32).astype(gates.dtype)
    g_cols = jnp.where(
        jnp.arange(LANE, dtype=jnp.int32)[None, :] == 0, send_g.reshape(-1, 1), jnp.zeros((), gates.dtype)
    )
    packed = jnp.concatenate([rows_xdy, g_cols], axis=1)
    row_width = packed.shape[1]
    packed = packed.reshape(axis_len, CAP * row_width // LANE, LANE)
    recv = expert_exchange(packed).reshape(axis_len, CAP, row_width)
    recv = jnp.transpose(recv, (1, 0, 2))
    gathered, other_gate, other_up, other_down = dp_gather(recv, gate_w, up_w, down_w)
    taken = own_flag == 1
    w_gate = jnp.where(taken, other_gate[0], gate_w[0])
    w_up = jnp.where(taken, other_up[0], up_w[0])
    w_down = jnp.where(taken, other_down[0], down_w[0])
    block_count = lax.axis_size("dp")
    row_x = gathered[:, :, :width]
    row_dy = gathered[:, :, width:2 * width]
    row_g = gathered[:, :, 2 * width:2 * width + 1]
    feature = (((2,), (0,)), ((), ()))
    rows_contract = (((0, 1), (0, 1)), ((), ()))
    hidden_count = w_gate.shape[1]
    w_both = jnp.concatenate([w_gate, w_up], axis=1)
    pre_both = lax.dot_general(row_x, w_both, feature, preferred_element_type=jnp.float32)
    pre_gate = pre_both[:, :, :hidden_count]
    pre_up = pre_both[:, :, hidden_count:]
    sigma = jax.nn.sigmoid(pre_gate)
    active = pre_gate * sigma
    hidden = (active * pre_up).astype(jnp.bfloat16)
    back = lax.dot_general(
        row_dy, w_down, (((2,), (1,)), ((), ())), preferred_element_type=jnp.float32
    )
    score = jnp.sum(hidden.astype(jnp.float32) * back, axis=2).T
    scaled = row_dy * row_g
    d_hidden = row_g.astype(jnp.float32) * back
    d_gate = (d_hidden * pre_up * sigma * (1.0 + pre_gate * (1.0 - sigma))).astype(jnp.bfloat16)
    d_up = (d_hidden * active).astype(jnp.bfloat16)
    d_both = jnp.concatenate([d_gate, d_up], axis=2)
    grad_both = lax.dot_general(row_x, d_both, rows_contract, preferred_element_type=jnp.float32)
    grad_gate = grad_both[:, :hidden_count]
    grad_up = grad_both[:, hidden_count:]
    grad_down = lax.dot_general(hidden, scaled, rows_contract, preferred_element_type=jnp.float32)
    scores = score.reshape(block_count, axis_len * CAP)
    parts = lax.all_to_all(scores, "dp", split_axis=0, concat_axis=0, tiled=True)
    own_scores = jnp.sum(parts, axis=0).reshape(axis_len, CAP)
    returned = lax.all_to_all(own_scores, "expert", split_axis=0, concat_axis=0, tiled=True)
    picked = jnp.sum(jnp.where(pick > 0, returned.reshape(1, -1), 0.0), axis=1)
    score_grad = jnp.where(valid, picked, 0.0).reshape(tok_count, top_count)
    out_gate = grad_gate.astype(jnp.bfloat16)[None]
    out_up = grad_up.astype(jnp.bfloat16)[None]
    out_down = grad_down.astype(jnp.bfloat16)[None]
    return (out_gate, out_up, out_down, score_grad)


def solution(mesh):
    placed = (
        P(("dp", "expert"), None),
        P(("dp", "expert"), None),
        P(("dp", "expert"), None),
        P(("dp", "expert"), None),
        P(),
        P("expert", None, "dp"),
        P("expert", None, "dp"),
        P("expert", "dp", None),
    )
    return jax.shard_map(
        body,
        mesh=mesh,
        in_specs=placed,
        out_specs=(
            P("expert", None, "dp"),
            P("expert", None, "dp"),
            P("expert", "dp", None),
            P(("dp", "expert"), None),
        ),
        check_vma=False,
    )
```

```python
import functools

import jax
import jax.numpy as jnp
from jax import lax
from jax.experimental import pallas as pl
from jax.experimental.pallas import tpu as pltpu
from jax.sharding import PartitionSpec as P

CAP = 6
LANE = 128


def partner(block, axis, stride):
    count = lax.axis_size(axis)
    route = []
    for low in range(count):
        high = low | 1 << stride
        if high != low and high < count:
            route += [(low, high), (high, low)]
    return lax.ppermute(block, axis, route)


def dp_gather_kernel(n_dp, ring, chunks, x_ref, o_ref, recv, recv_z, send):
    me = lax.axis_index("dp")
    ex = lax.axis_index("expert")
    rows = x_ref.shape[1]
    half = rows // 2
    piece = rows // chunks
    plane = me // ring
    pos = me % ring
    left = plane * ring + (pos + ring - 1) % ring
    right = plane * ring + (pos + 1) % ring
    far = plane * ring + (pos + 2) % ring
    across = (me + ring) % n_dp

    def span(k, start, size):
        return o_ref.at[:, pl.ds(k * rows + start, size), :]

    def push(src, dst, slot, sem, peer):
        copy = pltpu.make_async_remote_copy(
            src_ref=src,
            dst_ref=dst,
            send_sem=send.at[slot],
            recv_sem=sem,
            device_id=(peer, ex),
            device_id_type=pl.DeviceIdType.MESH,
        )
        copy.start()
        return copy

    def arrived(ref, sem):
        pltpu.make_async_copy(ref, ref, sem).wait()

    barrier = pltpu.get_barrier_semaphore()
    for peer in (left, right, across):
        pl.semaphore_signal(barrier, inc=1, device_id=(peer, ex), device_id_type=pl.DeviceIdType.MESH)
    pl.semaphore_wait(barrier, 3)

    local = pltpu.make_async_copy(x_ref, span(me, 0, rows), recv.at[me])
    local.start()
    sent = []
    for q in range(chunks):
        sent.append(
            push(
                x_ref.at[:, pl.ds(q * piece, piece), :],
                span(me, q * piece, piece),
                len(sent),
                recv_z.at[q],
                across,
            )
        )
    sent.append(push(x_ref, span(me, 0, rows), len(sent), recv.at[me], left))
    sent.append(push(x_ref, span(me, 0, rows), len(sent), recv.at[me], right))
    arrived(span(left, 0, rows), recv.at[left])
    sent.append(push(span(left, 0, half), span(left, 0, half), len(sent), recv.at[left], right))
    arrived(span(right, 0, rows), recv.at[right])
    sent.append(push(span(right, half, half), span(right, half, half), len(sent), recv.at[right], left))
    for q in range(chunks):
        chunk = span(across, q * piece, piece)
        arrived(chunk, recv_z.at[q])
        sent.append(push(chunk, chunk, len(sent), recv.at[across], left))
        sent.append(push(chunk, chunk, len(sent), recv.at[across], right))
    left_across = (left + ring) % n_dp
    right_across = (right + ring) % n_dp
    arrived(span(left_across, 0, rows), recv.at[left_across])
    sent.append(
        push(span(left_across, 0, half), span(left_across, 0, half), len(sent), recv.at[left_across], right)
    )
    arrived(span(right_across, 0, rows), recv.at[right_across])
    sent.append(
        push(span(right_across, half, half), span(right_across, half, half), len(sent), recv.at[right_across], left)
    )
    arrived(span(far, 0, rows), recv.at[far])
    far_across = (far + ring) % n_dp
    arrived(span(far_across, 0, rows), recv.at[far_across])
    local.wait()
    for copy in sent:
        copy.wait_send()


def dp_gather(block):
    n_dp = lax.axis_size("dp")
    ring = n_dp // 2
    chunks = 4
    cap, rows, row_width = block.shape
    sends = 3 * chunks + 6
    return pl.pallas_call(
        functools.partial(dp_gather_kernel, n_dp, ring, chunks),
        out_shape=jax.ShapeDtypeStruct((cap, n_dp * rows, row_width), block.dtype),
        in_specs=[pl.BlockSpec(memory_space=pl.ANY)],
        out_specs=pl.BlockSpec(memory_space=pl.ANY),
        scratch_shapes=[
            pltpu.SemaphoreType.DMA((n_dp,)),
            pltpu.SemaphoreType.DMA((chunks,)),
            pltpu.SemaphoreType.DMA((sends,)),
        ],
        compiler_params=pltpu.CompilerParams(collective_id=0, has_side_effects=True),
    )(block)


def expert_exchange_kernel(n_ex, x_ref, wg_ref, o_ref, og_ref, recv, send, local_sem, recv_w):
    me = lax.axis_index("expert")
    dp = lax.axis_index("dp")
    barrier = pltpu.get_barrier_semaphore()
    for step in range(1, n_ex):
        peer = (me + step) % n_ex
        pl.semaphore_signal(barrier, inc=1, device_id=(dp, peer), device_id_type=pl.DeviceIdType.MESH)
    pl.semaphore_wait(barrier, n_ex - 1)
    local = pltpu.make_async_copy(x_ref.at[pl.ds(me, 1)], o_ref.at[pl.ds(me, 1)], local_sem.at[0])
    local.start()
    sent = []
    for step in range(1, n_ex):
        peer = (me + step) % n_ex
        copy = pltpu.make_async_remote_copy(
            src_ref=x_ref.at[pl.ds(peer, 1)],
            dst_ref=o_ref.at[pl.ds(me, 1)],
            send_sem=send.at[step],
            recv_sem=recv.at[0],
            device_id=(dp, peer),
            device_id_type=pl.DeviceIdType.MESH,
        )
        copy.start()
        sent.append(copy)
    swap = pltpu.make_async_remote_copy(
        src_ref=wg_ref,
        dst_ref=og_ref,
        send_sem=send.at[0],
        recv_sem=recv_w.at[0],
        device_id=(dp, (me + n_ex // 2) % n_ex),
        device_id_type=pl.DeviceIdType.MESH,
    )
    swap.start()
    pltpu.make_async_copy(
        x_ref.at[pl.ds(0, n_ex - 1)], o_ref.at[pl.ds(0, n_ex - 1)], recv.at[0]
    ).wait()
    local.wait()
    for copy in sent:
        copy.wait_send()
    swap.wait()


def expert_exchange(block, w_gate):
    n_ex = lax.axis_size("expert")
    return pl.pallas_call(
        functools.partial(expert_exchange_kernel, n_ex),
        out_shape=(
            jax.ShapeDtypeStruct(block.shape, block.dtype),
            jax.ShapeDtypeStruct(w_gate.shape, w_gate.dtype),
        ),
        in_specs=[pl.BlockSpec(memory_space=pl.ANY)] * 2,
        out_specs=(pl.BlockSpec(memory_space=pl.ANY),) * 2,
        scratch_shapes=[
            pltpu.SemaphoreType.DMA((1,)),
            pltpu.SemaphoreType.DMA((n_ex,)),
            pltpu.SemaphoreType.DMA((1,)),
            pltpu.SemaphoreType.DMA((1,)),
        ],
        compiler_params=pltpu.CompilerParams(collective_id=1, has_side_effects=True),
    )(block, w_gate)


def body(tokens, cotangent, expert_ids, gates, swap_flags, gate_w, up_w, down_w):
    axis_len = lax.axis_size("expert")
    half_axis = axis_len // 2
    pair_bit = axis_len.bit_length() - 2
    own_slot = lax.axis_index("expert")
    tok_count = tokens.shape[0]
    top_count = expert_ids.shape[1]
    width = tokens.shape[1]
    flat_ids = expert_ids.reshape(-1)
    choice_count = flat_ids.shape[0]
    valid = flat_ids < axis_len
    pair_index = jnp.arange(half_axis, dtype=jnp.int32)
    flag_of = jnp.sum(
        jnp.where((flat_ids % half_axis)[:, None] == pair_index[None, :], swap_flags[None, :], 0),
        axis=1,
    )
    own_flag = jnp.sum(jnp.where(pair_index == own_slot % half_axis, swap_flags, 0))
    target = jnp.where(flag_of == 1, jnp.bitwise_xor(flat_ids, half_axis), flat_ids)
    target = jnp.where(valid, target, 0)
    onehot = (
        (target[:, None] == jnp.arange(axis_len, dtype=jnp.int32)[None, :]) & valid[:, None]
    ).astype(jnp.bfloat16)
    order = jnp.arange(choice_count, dtype=jnp.int32)
    lower = (order[None, :] <= order[:, None]).astype(jnp.bfloat16)
    counts = jnp.dot(lower, onehot, preferred_element_type=jnp.float32)
    ranks = jnp.sum(counts * onehot.astype(jnp.float32), axis=1).astype(jnp.int32) - 1
    slot_count = axis_len * CAP
    slots = jnp.where(valid, target * CAP + ranks, slot_count)
    pick = (slots[:, None] == jnp.arange(slot_count, dtype=jnp.int32)[None, :]).astype(jnp.bfloat16)
    token_pick = jnp.sum(pick.reshape(tok_count, top_count, slot_count).astype(jnp.float32), axis=1)
    token_pick = token_pick.astype(jnp.bfloat16)
    rows_xdy = lax.dot_general(
        token_pick,
        jnp.concatenate([tokens, cotangent], axis=1),
        (((0,), (0,)), ((), ())),
        preferred_element_type=jnp.float32,
    ).astype(tokens.dtype)
    send_g = jnp.dot(gates.reshape(1, -1), pick, preferred_element_type=jnp.float32).astype(gates.dtype)
    g_cols = jnp.where(
        jnp.arange(LANE, dtype=jnp.int32)[None, :] == 0, send_g.reshape(-1, 1), jnp.zeros((), gates.dtype)
    )
    packed = jnp.concatenate([rows_xdy, g_cols], axis=1)
    row_width = packed.shape[1]
    packed = packed.reshape(axis_len, CAP * row_width // LANE, LANE)
    recv, other_gate = expert_exchange(packed, gate_w)
    recv = recv.reshape(axis_len, CAP, row_width)
    recv = jnp.transpose(recv, (1, 0, 2))
    recv, up_w, down_w = lax.optimization_barrier((recv, up_w, down_w))
    w_gate = gate_w[0]
    w_up = up_w[0]
    w_down = down_w[0]
    other_up, other_down = partner((up_w, down_w), "expert", pair_bit)
    taken = own_flag == 1
    w_gate = jnp.where(taken, other_gate[0], w_gate)
    w_up = jnp.where(taken, other_up[0], w_up)
    w_down = jnp.where(taken, other_down[0], w_down)
    gathered = dp_gather(recv)
    block_count = lax.axis_size("dp")
    row_x = gathered[:, :, :width]
    row_dy = gathered[:, :, width:2 * width]
    row_g = gathered[:, :, 2 * width:2 * width + 1]
    feature = (((2,), (0,)), ((), ()))
    rows_contract = (((0, 1), (0, 1)), ((), ()))
    hidden_count = w_gate.shape[1]
    w_both = jnp.concatenate([w_gate, w_up], axis=1)
    pre_both = lax.dot_general(row_x, w_both, feature, preferred_element_type=jnp.float32)
    pre_gate = pre_both[:, :, :hidden_count]
    pre_up = pre_both[:, :, hidden_count:]
    sigma = jax.nn.sigmoid(pre_gate)
    active = pre_gate * sigma
    hidden = (active * pre_up).astype(jnp.bfloat16)
    back = lax.dot_general(
        row_dy, w_down, (((2,), (1,)), ((), ())), preferred_element_type=jnp.float32
    )
    score = jnp.sum(hidden.astype(jnp.float32) * back, axis=2).T
    scaled = row_dy * row_g
    d_hidden = row_g.astype(jnp.float32) * back
    d_gate = (d_hidden * pre_up * sigma * (1.0 + pre_gate * (1.0 - sigma))).astype(jnp.bfloat16)
    d_up = (d_hidden * active).astype(jnp.bfloat16)
    d_both = jnp.concatenate([d_gate, d_up], axis=2)
    grad_both = lax.dot_general(row_x, d_both, rows_contract, preferred_element_type=jnp.float32)
    grad_gate = grad_both[:, :hidden_count]
    grad_up = grad_both[:, hidden_count:]
    grad_down = lax.dot_general(hidden, scaled, rows_contract, preferred_element_type=jnp.float32)
    scores = score.reshape(block_count, axis_len * CAP)
    parts = lax.all_to_all(scores, "dp", split_axis=0, concat_axis=0, tiled=True)
    own_scores = jnp.sum(parts, axis=0).reshape(axis_len, CAP)
    returned = lax.all_to_all(own_scores, "expert", split_axis=0, concat_axis=0, tiled=True)
    picked = jnp.sum(jnp.where(pick > 0, returned.reshape(1, -1), 0.0), axis=1)
    score_grad = jnp.where(valid, picked, 0.0).reshape(tok_count, top_count)
    out_gate = grad_gate.astype(jnp.bfloat16)[None]
    out_up = grad_up.astype(jnp.bfloat16)[None]
    out_down = grad_down.astype(jnp.bfloat16)[None]
    return (out_gate, out_up, out_down, score_grad)


def solution(mesh):
    placed = (
        P(("dp", "expert"), None),
        P(("dp", "expert"), None),
        P(("dp", "expert"), None),
        P(("dp", "expert"), None),
        P(),
        P("expert", None, "dp"),
        P("expert", None, "dp"),
        P("expert", "dp", None),
    )
    return jax.shard_map(
        body,
        mesh=mesh,
        in_specs=placed,
        out_specs=(
            P("expert", None, "dp"),
            P("expert", None, "dp"),
            P("expert", "dp", None),
            P(("dp", "expert"), None),
        ),
        check_vma=False,
    )
```

```python
import functools

import jax
import jax.numpy as jnp
from jax import lax
from jax.experimental import pallas as pl
from jax.experimental.pallas import tpu as pltpu
from jax.sharding import PartitionSpec as P

CAP = 6
LANE = 128


def partner(block, axis, stride):
    count = lax.axis_size(axis)
    route = []
    for low in range(count):
        high = low | 1 << stride
        if high != low and high < count:
            route += [(low, high), (high, low)]
    return lax.ppermute(block, axis, route)


def dp_gather_kernel(n_dp, ring, chunks, x_ref, o_ref, recv, recv_z, send):
    me = lax.axis_index("dp")
    ex = lax.axis_index("expert")
    rows = x_ref.shape[1]
    half = rows // 2
    piece = rows // chunks
    plane = me // ring
    pos = me % ring
    left = plane * ring + (pos + ring - 1) % ring
    right = plane * ring + (pos + 1) % ring
    far = plane * ring + (pos + 2) % ring
    across = (me + ring) % n_dp

    def span(k, start, size):
        return o_ref.at[:, pl.ds(k * rows + start, size), :]

    def push(src, dst, slot, sem, peer):
        copy = pltpu.make_async_remote_copy(
            src_ref=src,
            dst_ref=dst,
            send_sem=send.at[slot],
            recv_sem=sem,
            device_id=(peer, ex),
            device_id_type=pl.DeviceIdType.MESH,
        )
        copy.start()
        return copy

    def arrived(ref, sem):
        pltpu.make_async_copy(ref, ref, sem).wait()

    barrier = pltpu.get_barrier_semaphore()
    for peer in (left, right, across):
        pl.semaphore_signal(barrier, inc=1, device_id=(peer, ex), device_id_type=pl.DeviceIdType.MESH)
    pl.semaphore_wait(barrier, 3)

    sent = []
    for q in range(chunks):
        sent.append(
            push(
                x_ref.at[:, pl.ds(q * piece, piece), :],
                span(me, q * piece, piece),
                len(sent),
                recv_z.at[q],
                across,
            )
        )
    sent.append(push(x_ref, span(me, 0, rows), len(sent), recv.at[me], left))
    sent.append(push(x_ref, span(me, 0, rows), len(sent), recv.at[me], right))
    arrived(span(left, 0, rows), recv.at[left])
    sent.append(push(span(left, 0, half), span(left, 0, half), len(sent), recv.at[left], right))
    arrived(span(right, 0, rows), recv.at[right])
    sent.append(push(span(right, half, half), span(right, half, half), len(sent), recv.at[right], left))
    for q in range(chunks):
        chunk = span(across, q * piece, piece)
        arrived(chunk, recv_z.at[q])
        sent.append(push(chunk, chunk, len(sent), recv.at[across], left))
        sent.append(push(chunk, chunk, len(sent), recv.at[across], right))
    left_across = (left + ring) % n_dp
    right_across = (right + ring) % n_dp
    arrived(span(left_across, 0, rows), recv.at[left_across])
    sent.append(
        push(span(left_across, 0, half), span(left_across, 0, half), len(sent), recv.at[left_across], right)
    )
    arrived(span(right_across, 0, rows), recv.at[right_across])
    sent.append(
        push(span(right_across, half, half), span(right_across, half, half), len(sent), recv.at[right_across], left)
    )
    local = pltpu.make_async_copy(x_ref, span(me, 0, rows), recv.at[me])
    local.start()
    arrived(span(far, 0, rows), recv.at[far])
    far_across = (far + ring) % n_dp
    arrived(span(far_across, 0, rows), recv.at[far_across])
    local.wait()
    for copy in sent:
        copy.wait_send()


def dp_gather(block):
    n_dp = lax.axis_size("dp")
    ring = n_dp // 2
    chunks = 4
    cap, rows, row_width = block.shape
    sends = 3 * chunks + 6
    return pl.pallas_call(
        functools.partial(dp_gather_kernel, n_dp, ring, chunks),
        out_shape=jax.ShapeDtypeStruct((cap, n_dp * rows, row_width), block.dtype),
        in_specs=[pl.BlockSpec(memory_space=pl.ANY)],
        out_specs=pl.BlockSpec(memory_space=pl.ANY),
        scratch_shapes=[
            pltpu.SemaphoreType.DMA((n_dp,)),
            pltpu.SemaphoreType.DMA((chunks,)),
            pltpu.SemaphoreType.DMA((sends,)),
        ],
        compiler_params=pltpu.CompilerParams(collective_id=0, has_side_effects=True),
    )(block)


def expert_exchange_kernel(n_ex, x_ref, o_ref, recv, send, local_sem):
    me = lax.axis_index("expert")
    dp = lax.axis_index("dp")
    barrier = pltpu.get_barrier_semaphore()
    for step in range(1, n_ex):
        peer = (me + step) % n_ex
        pl.semaphore_signal(barrier, inc=1, device_id=(dp, peer), device_id_type=pl.DeviceIdType.MESH)
    pl.semaphore_wait(barrier, n_ex - 1)
    local = pltpu.make_async_copy(x_ref.at[pl.ds(me, 1)], o_ref.at[pl.ds(me, 1)], local_sem.at[0])
    local.start()
    sent = []
    for step in range(1, n_ex):
        peer = (me + step) % n_ex
        copy = pltpu.make_async_remote_copy(
            src_ref=x_ref.at[pl.ds(peer, 1)],
            dst_ref=o_ref.at[pl.ds(me, 1)],
            send_sem=send.at[step],
            recv_sem=recv.at[0],
            device_id=(dp, peer),
            device_id_type=pl.DeviceIdType.MESH,
        )
        copy.start()
        sent.append(copy)
    pltpu.make_async_copy(
        x_ref.at[pl.ds(0, n_ex - 1)], o_ref.at[pl.ds(0, n_ex - 1)], recv.at[0]
    ).wait()
    local.wait()
    for copy in sent:
        copy.wait_send()


def expert_exchange(block):
    n_ex = lax.axis_size("expert")
    return pl.pallas_call(
        functools.partial(expert_exchange_kernel, n_ex),
        out_shape=jax.ShapeDtypeStruct(block.shape, block.dtype),
        in_specs=[pl.BlockSpec(memory_space=pl.ANY)],
        out_specs=pl.BlockSpec(memory_space=pl.ANY),
        scratch_shapes=[
            pltpu.SemaphoreType.DMA((1,)),
            pltpu.SemaphoreType.DMA((n_ex,)),
            pltpu.SemaphoreType.DMA((1,)),
        ],
        compiler_params=pltpu.CompilerParams(collective_id=1, has_side_effects=True),
    )(block)


def body(tokens, cotangent, expert_ids, gates, swap_flags, gate_w, up_w, down_w):
    axis_len = lax.axis_size("expert")
    half_axis = axis_len // 2
    pair_bit = axis_len.bit_length() - 2
    own_slot = lax.axis_index("expert")
    tok_count = tokens.shape[0]
    top_count = expert_ids.shape[1]
    width = tokens.shape[1]
    flat_ids = expert_ids.reshape(-1)
    choice_count = flat_ids.shape[0]
    valid = flat_ids < axis_len
    pair_index = jnp.arange(half_axis, dtype=jnp.int32)
    flag_of = jnp.sum(
        jnp.where((flat_ids % half_axis)[:, None] == pair_index[None, :], swap_flags[None, :], 0),
        axis=1,
    )
    own_flag = jnp.sum(jnp.where(pair_index == own_slot % half_axis, swap_flags, 0))
    target = jnp.where(flag_of == 1, jnp.bitwise_xor(flat_ids, half_axis), flat_ids)
    target = jnp.where(valid, target, 0)
    onehot = (
        (target[:, None] == jnp.arange(axis_len, dtype=jnp.int32)[None, :]) & valid[:, None]
    ).astype(jnp.bfloat16)
    order = jnp.arange(choice_count, dtype=jnp.int32)
    lower = (order[None, :] <= order[:, None]).astype(jnp.bfloat16)
    counts = jnp.dot(lower, onehot, preferred_element_type=jnp.float32)
    ranks = jnp.sum(counts * onehot.astype(jnp.float32), axis=1).astype(jnp.int32) - 1
    slot_count = axis_len * CAP
    slots = jnp.where(valid, target * CAP + ranks, slot_count)
    pick = (slots[:, None] == jnp.arange(slot_count, dtype=jnp.int32)[None, :]).astype(jnp.bfloat16)
    token_pick = jnp.sum(pick.reshape(tok_count, top_count, slot_count).astype(jnp.float32), axis=1)
    token_pick = token_pick.astype(jnp.bfloat16)
    rows_xdy = lax.dot_general(
        token_pick,
        jnp.concatenate([tokens, cotangent], axis=1),
        (((0,), (0,)), ((), ())),
        preferred_element_type=jnp.float32,
    ).astype(tokens.dtype)
    send_g = jnp.dot(gates.reshape(1, -1), pick, preferred_element_type=jnp.float32).astype(gates.dtype)
    g_cols = jnp.where(
        jnp.arange(LANE, dtype=jnp.int32)[None, :] == 0, send_g.reshape(-1, 1), jnp.zeros((), gates.dtype)
    )
    packed = jnp.concatenate([rows_xdy, g_cols], axis=1)
    row_width = packed.shape[1]
    packed = packed.reshape(axis_len, CAP * row_width // LANE, LANE)
    recv = expert_exchange(packed).reshape(axis_len, CAP, row_width)
    recv = jnp.transpose(recv, (1, 0, 2))
    recv, gate_w, up_w, down_w = lax.optimization_barrier((recv, gate_w, up_w, down_w))
    w_gate = gate_w[0]
    w_up = up_w[0]
    w_down = down_w[0]
    other_gate, other_up, other_down = partner((gate_w, up_w, down_w), "expert", pair_bit)
    taken = own_flag == 1
    w_gate = jnp.where(taken, other_gate[0], w_gate)
    w_up = jnp.where(taken, other_up[0], w_up)
    w_down = jnp.where(taken, other_down[0], w_down)
    gathered = dp_gather(recv)
    block_count = lax.axis_size("dp")
    row_x = gathered[:, :, :width]
    row_dy = gathered[:, :, width:2 * width]
    row_g = gathered[:, :, 2 * width:2 * width + 1]
    feature = (((2,), (0,)), ((), ()))
    rows_contract = (((0, 1), (0, 1)), ((), ()))
    hidden_count = w_gate.shape[1]
    w_both = jnp.concatenate([w_gate, w_up], axis=1)
    pre_both = lax.dot_general(row_x, w_both, feature, preferred_element_type=jnp.float32)
    pre_gate = pre_both[:, :, :hidden_count]
    pre_up = pre_both[:, :, hidden_count:]
    sigma = jax.nn.sigmoid(pre_gate)
    active = pre_gate * sigma
    hidden = (active * pre_up).astype(jnp.bfloat16)
    back = lax.dot_general(
        row_dy, w_down, (((2,), (1,)), ((), ())), preferred_element_type=jnp.float32
    )
    score = jnp.sum(hidden.astype(jnp.float32) * back, axis=2).T
    scaled = row_dy * row_g
    d_hidden = row_g.astype(jnp.float32) * back
    d_gate = (d_hidden * pre_up * sigma * (1.0 + pre_gate * (1.0 - sigma))).astype(jnp.bfloat16)
    d_up = (d_hidden * active).astype(jnp.bfloat16)
    d_both = jnp.concatenate([d_gate, d_up], axis=2)
    grad_both = lax.dot_general(row_x, d_both, rows_contract, preferred_element_type=jnp.float32)
    grad_gate = grad_both[:, :hidden_count]
    grad_up = grad_both[:, hidden_count:]
    grad_down = lax.dot_general(hidden, scaled, rows_contract, preferred_element_type=jnp.float32)
    scores = score.reshape(block_count, axis_len * CAP)
    parts = lax.all_to_all(scores, "dp", split_axis=0, concat_axis=0, tiled=True)
    own_scores = jnp.sum(parts, axis=0).reshape(axis_len, CAP)
    returned = lax.all_to_all(own_scores, "expert", split_axis=0, concat_axis=0, tiled=True)
    picked = jnp.sum(jnp.where(pick > 0, returned.reshape(1, -1), 0.0), axis=1)
    score_grad = jnp.where(valid, picked, 0.0).reshape(tok_count, top_count)
    out_gate = grad_gate.astype(jnp.bfloat16)[None]
    out_up = grad_up.astype(jnp.bfloat16)[None]
    out_down = grad_down.astype(jnp.bfloat16)[None]
    return (out_gate, out_up, out_down, score_grad)


def solution(mesh):
    placed = (
        P(("dp", "expert"), None),
        P(("dp", "expert"), None),
        P(("dp", "expert"), None),
        P(("dp", "expert"), None),
        P(),
        P("expert", None, "dp"),
        P("expert", None, "dp"),
        P("expert", "dp", None),
    )
    return jax.shard_map(
        body,
        mesh=mesh,
        in_specs=placed,
        out_specs=(
            P("expert", None, "dp"),
            P("expert", None, "dp"),
            P("expert", "dp", None),
            P(("dp", "expert"), None),
        ),
        check_vma=False,
    )
```

```python
import functools

import jax
import jax.numpy as jnp
from jax import lax
from jax.experimental import pallas as pl
from jax.experimental.pallas import tpu as pltpu
from jax.sharding import PartitionSpec as P

CAP = 6
LANE = 128


def partner(block, axis, stride):
    count = lax.axis_size(axis)
    route = []
    for low in range(count):
        high = low | 1 << stride
        if high != low and high < count:
            route += [(low, high), (high, low)]
    return lax.ppermute(block, axis, route)


def dp_gather_kernel(n_dp, ring, chunks, x_ref, o_ref, recv, recv_z, send):
    me = lax.axis_index("dp")
    ex = lax.axis_index("expert")
    rows = x_ref.shape[1]
    half = rows // 2
    piece = rows // chunks
    plane = me // ring
    pos = me % ring
    left = plane * ring + (pos + ring - 1) % ring
    right = plane * ring + (pos + 1) % ring
    far = plane * ring + (pos + 2) % ring
    across = (me + ring) % n_dp

    def span(k, start, size):
        return o_ref.at[:, pl.ds(k * rows + start, size), :]

    def push(src, dst, slot, sem, peer):
        copy = pltpu.make_async_remote_copy(
            src_ref=src,
            dst_ref=dst,
            send_sem=send.at[slot],
            recv_sem=sem,
            device_id=(peer, ex),
            device_id_type=pl.DeviceIdType.MESH,
        )
        copy.start()
        return copy

    def arrived(ref, sem):
        pltpu.make_async_copy(ref, ref, sem).wait()

    barrier = pltpu.get_barrier_semaphore()
    for peer in (left, right, across):
        pl.semaphore_signal(barrier, inc=1, device_id=(peer, ex), device_id_type=pl.DeviceIdType.MESH)
    pl.semaphore_wait(barrier, 3)

    sent = []
    for q in range(chunks):
        sent.append(
            push(
                x_ref.at[:, pl.ds(q * piece, piece), :],
                span(me, q * piece, piece),
                len(sent),
                recv_z.at[q],
                across,
            )
        )
    sent.append(push(x_ref, span(me, 0, rows), len(sent), recv.at[me], left))
    sent.append(push(x_ref, span(me, 0, rows), len(sent), recv.at[me], right))
    local = pltpu.make_async_copy(x_ref, span(me, 0, rows), recv.at[me])
    local.start()
    arrived(span(left, 0, rows), recv.at[left])
    sent.append(push(span(left, 0, half), span(left, 0, half), len(sent), recv.at[left], right))
    arrived(span(right, 0, rows), recv.at[right])
    sent.append(push(span(right, half, half), span(right, half, half), len(sent), recv.at[right], left))
    for q in range(chunks):
        chunk = span(across, q * piece, piece)
        arrived(chunk, recv_z.at[q])
        sent.append(push(chunk, chunk, len(sent), recv.at[across], left))
        sent.append(push(chunk, chunk, len(sent), recv.at[across], right))
    left_across = (left + ring) % n_dp
    right_across = (right + ring) % n_dp
    arrived(span(left_across, 0, rows), recv.at[left_across])
    sent.append(
        push(span(left_across, 0, half), span(left_across, 0, half), len(sent), recv.at[left_across], right)
    )
    arrived(span(right_across, 0, rows), recv.at[right_across])
    sent.append(
        push(span(right_across, half, half), span(right_across, half, half), len(sent), recv.at[right_across], left)
    )
    arrived(span(far, 0, rows), recv.at[far])
    far_across = (far + ring) % n_dp
    arrived(span(far_across, 0, rows), recv.at[far_across])
    local.wait()
    for copy in sent:
        copy.wait_send()


def dp_gather(block):
    n_dp = lax.axis_size("dp")
    ring = n_dp // 2
    chunks = 4
    cap, rows, row_width = block.shape
    sends = 3 * chunks + 6
    return pl.pallas_call(
        functools.partial(dp_gather_kernel, n_dp, ring, chunks),
        out_shape=jax.ShapeDtypeStruct((cap, n_dp * rows, row_width), block.dtype),
        in_specs=[pl.BlockSpec(memory_space=pl.ANY)],
        out_specs=pl.BlockSpec(memory_space=pl.ANY),
        scratch_shapes=[
            pltpu.SemaphoreType.DMA((n_dp,)),
            pltpu.SemaphoreType.DMA((chunks,)),
            pltpu.SemaphoreType.DMA((sends,)),
        ],
        compiler_params=pltpu.CompilerParams(collective_id=0, has_side_effects=True),
    )(block)


def expert_exchange_kernel(n_ex, x_ref, o_ref, recv, send, local_sem):
    me = lax.axis_index("expert")
    dp = lax.axis_index("dp")
    barrier = pltpu.get_barrier_semaphore()
    for step in range(1, n_ex):
        peer = (me + step) % n_ex
        pl.semaphore_signal(barrier, inc=1, device_id=(dp, peer), device_id_type=pl.DeviceIdType.MESH)
    pl.semaphore_wait(barrier, n_ex - 1)
    local = pltpu.make_async_copy(x_ref.at[pl.ds(me, 1)], o_ref.at[pl.ds(me, 1)], local_sem.at[0])
    local.start()
    sent = []
    for step in range(1, n_ex):
        peer = (me + step) % n_ex
        copy = pltpu.make_async_remote_copy(
            src_ref=x_ref.at[pl.ds(peer, 1)],
            dst_ref=o_ref.at[pl.ds(me, 1)],
            send_sem=send.at[step],
            recv_sem=recv.at[0],
            device_id=(dp, peer),
            device_id_type=pl.DeviceIdType.MESH,
        )
        copy.start()
        sent.append(copy)
    pltpu.make_async_copy(
        x_ref.at[pl.ds(0, n_ex - 1)], o_ref.at[pl.ds(0, n_ex - 1)], recv.at[0]
    ).wait()
    local.wait()
    for copy in sent:
        copy.wait_send()


def expert_exchange(block):
    n_ex = lax.axis_size("expert")
    return pl.pallas_call(
        functools.partial(expert_exchange_kernel, n_ex),
        out_shape=jax.ShapeDtypeStruct(block.shape, block.dtype),
        in_specs=[pl.BlockSpec(memory_space=pl.ANY)],
        out_specs=pl.BlockSpec(memory_space=pl.ANY),
        scratch_shapes=[
            pltpu.SemaphoreType.DMA((1,)),
            pltpu.SemaphoreType.DMA((n_ex,)),
            pltpu.SemaphoreType.DMA((1,)),
        ],
        compiler_params=pltpu.CompilerParams(collective_id=1, has_side_effects=True),
    )(block)


def body(tokens, cotangent, expert_ids, gates, swap_flags, gate_w, up_w, down_w):
    axis_len = lax.axis_size("expert")
    half_axis = axis_len // 2
    pair_bit = axis_len.bit_length() - 2
    own_slot = lax.axis_index("expert")
    tok_count = tokens.shape[0]
    top_count = expert_ids.shape[1]
    width = tokens.shape[1]
    flat_ids = expert_ids.reshape(-1)
    choice_count = flat_ids.shape[0]
    valid = flat_ids < axis_len
    pair_index = jnp.arange(half_axis, dtype=jnp.int32)
    flag_of = jnp.sum(
        jnp.where((flat_ids % half_axis)[:, None] == pair_index[None, :], swap_flags[None, :], 0),
        axis=1,
    )
    own_flag = jnp.sum(jnp.where(pair_index == own_slot % half_axis, swap_flags, 0))
    target = jnp.where(flag_of == 1, jnp.bitwise_xor(flat_ids, half_axis), flat_ids)
    target = jnp.where(valid, target, 0)
    onehot = (
        (target[:, None] == jnp.arange(axis_len, dtype=jnp.int32)[None, :]) & valid[:, None]
    ).astype(jnp.bfloat16)
    order = jnp.arange(choice_count, dtype=jnp.int32)
    lower = (order[None, :] <= order[:, None]).astype(jnp.bfloat16)
    counts = jnp.dot(lower, onehot, preferred_element_type=jnp.float32)
    ranks = jnp.sum(counts * onehot.astype(jnp.float32), axis=1).astype(jnp.int32) - 1
    slot_count = axis_len * CAP
    slots = jnp.where(valid, target * CAP + ranks, slot_count)
    pick = (slots[:, None] == jnp.arange(slot_count, dtype=jnp.int32)[None, :]).astype(jnp.bfloat16)
    token_pick = jnp.sum(pick.reshape(tok_count, top_count, slot_count).astype(jnp.float32), axis=1)
    token_pick = token_pick.astype(jnp.bfloat16)
    rows_xdy = lax.dot_general(
        token_pick,
        jnp.concatenate([tokens, cotangent], axis=1),
        (((0,), (0,)), ((), ())),
        preferred_element_type=jnp.float32,
    ).astype(tokens.dtype)
    send_g = jnp.dot(gates.reshape(1, -1), pick, preferred_element_type=jnp.float32).astype(gates.dtype)
    g_cols = jnp.where(
        jnp.arange(LANE, dtype=jnp.int32)[None, :] == 0, send_g.reshape(-1, 1), jnp.zeros((), gates.dtype)
    )
    packed = jnp.concatenate([rows_xdy, g_cols], axis=1)
    row_width = packed.shape[1]
    packed = packed.reshape(axis_len, CAP * row_width // LANE, LANE)
    recv = expert_exchange(packed).reshape(axis_len, CAP, row_width)
    recv = jnp.transpose(recv, (1, 0, 2))
    recv, gate_w, up_w, down_w = lax.optimization_barrier((recv, gate_w, up_w, down_w))
    w_gate = gate_w[0]
    w_up = up_w[0]
    w_down = down_w[0]
    other_gate, other_up, other_down = partner((gate_w, up_w, down_w), "expert", pair_bit)
    taken = own_flag == 1
    w_gate = jnp.where(taken, other_gate[0], w_gate)
    w_up = jnp.where(taken, other_up[0], w_up)
    w_down = jnp.where(taken, other_down[0], w_down)
    gathered = dp_gather(recv)
    block_count = lax.axis_size("dp")
    row_x = gathered[:, :, :width]
    row_dy = gathered[:, :, width:2 * width]
    row_g = gathered[:, :, 2 * width:2 * width + 1]
    feature = (((2,), (0,)), ((), ()))
    rows_contract = (((0, 1), (0, 1)), ((), ()))
    hidden_count = w_gate.shape[1]
    w_both = jnp.concatenate([w_gate, w_up], axis=1)
    pre_both = lax.dot_general(row_x, w_both, feature, preferred_element_type=jnp.float32)
    pre_gate = pre_both[:, :, :hidden_count]
    pre_up = pre_both[:, :, hidden_count:]
    sigma = jax.nn.sigmoid(pre_gate)
    active = pre_gate * sigma
    hidden = (active * pre_up).astype(jnp.bfloat16)
    back = lax.dot_general(
        row_dy, w_down, (((2,), (1,)), ((), ())), preferred_element_type=jnp.float32
    )
    score = jnp.sum(hidden.astype(jnp.float32) * back, axis=2).T
    scaled = row_dy * row_g
    d_hidden = row_g.astype(jnp.float32) * back
    d_gate = (d_hidden * pre_up * sigma * (1.0 + pre_gate * (1.0 - sigma))).astype(jnp.bfloat16)
    d_up = (d_hidden * active).astype(jnp.bfloat16)
    d_both = jnp.concatenate([d_gate, d_up], axis=2)
    grad_both = lax.dot_general(row_x, d_both, rows_contract, preferred_element_type=jnp.float32)
    grad_gate = grad_both[:, :hidden_count]
    grad_up = grad_both[:, hidden_count:]
    grad_down = lax.dot_general(hidden, scaled, rows_contract, preferred_element_type=jnp.float32)
    scores = score.reshape(block_count, axis_len * CAP)
    parts = lax.all_to_all(scores, "dp", split_axis=0, concat_axis=0, tiled=True)
    own_scores = jnp.sum(parts, axis=0).reshape(axis_len, CAP)
    returned = lax.all_to_all(own_scores, "expert", split_axis=0, concat_axis=0, tiled=True)
    picked = jnp.sum(jnp.where(pick > 0, returned.reshape(1, -1), 0.0), axis=1)
    score_grad = jnp.where(valid, picked, 0.0).reshape(tok_count, top_count)
    out_gate = grad_gate.astype(jnp.bfloat16)[None]
    out_up = grad_up.astype(jnp.bfloat16)[None]
    out_down = grad_down.astype(jnp.bfloat16)[None]
    return (out_gate, out_up, out_down, score_grad)


def solution(mesh):
    placed = (
        P(("dp", "expert"), None),
        P(("dp", "expert"), None),
        P(("dp", "expert"), None),
        P(("dp", "expert"), None),
        P(),
        P("expert", None, "dp"),
        P("expert", None, "dp"),
        P("expert", "dp", None),
    )
    return jax.shard_map(
        body,
        mesh=mesh,
        in_specs=placed,
        out_specs=(
            P("expert", None, "dp"),
            P("expert", None, "dp"),
            P("expert", "dp", None),
            P(("dp", "expert"), None),
        ),
        check_vma=False,
    )
```

```python
import functools

import jax
import jax.numpy as jnp
from jax import lax
from jax.experimental import pallas as pl
from jax.experimental.pallas import tpu as pltpu
from jax.sharding import PartitionSpec as P

CAP = 6
LANE = 128


def partner(block, axis, stride):
    count = lax.axis_size(axis)
    route = []
    for low in range(count):
        high = low | 1 << stride
        if high != low and high < count:
            route += [(low, high), (high, low)]
    return lax.ppermute(block, axis, route)


def dp_gather_kernel(n_dp, ring, chunks, x_ref, o_ref, recv, recv_z, send, stage, stage_sem):
    me = lax.axis_index("dp")
    ex = lax.axis_index("expert")
    rows = x_ref.shape[1]
    half = rows // 2
    piece = rows // chunks
    plane = me // ring
    pos = me % ring
    left = plane * ring + (pos + ring - 1) % ring
    right = plane * ring + (pos + 1) % ring
    far = plane * ring + (pos + 2) % ring
    across = (me + ring) % n_dp

    def span(k, start, size):
        return o_ref.at[:, pl.ds(k * rows + start, size), :]

    def push(src, dst, slot, sem, peer):
        copy = pltpu.make_async_remote_copy(
            src_ref=src,
            dst_ref=dst,
            send_sem=send.at[slot],
            recv_sem=sem,
            device_id=(peer, ex),
            device_id_type=pl.DeviceIdType.MESH,
        )
        copy.start()
        return copy

    def arrived(ref, sem):
        pltpu.make_async_copy(ref, ref, sem).wait()

    barrier = pltpu.get_barrier_semaphore()
    for peer in (left, right, across):
        pl.semaphore_signal(barrier, inc=1, device_id=(peer, ex), device_id_type=pl.DeviceIdType.MESH)
    pl.semaphore_wait(barrier, 3)

    sent = []
    for q in range(chunks):
        sent.append(
            push(
                x_ref.at[:, pl.ds(q * piece, piece), :],
                span(me, q * piece, piece),
                len(sent),
                recv_z.at[q],
                across,
            )
        )
    sent.append(push(x_ref, span(me, 0, rows), len(sent), recv.at[me], left))
    sent.append(push(x_ref, span(me, 0, rows), len(sent), recv.at[me], right))
    staged = pltpu.make_async_copy(x_ref, stage, stage_sem.at[0])
    staged.start()
    staged.wait()
    local = pltpu.make_async_copy(stage, span(me, 0, rows), recv.at[me])
    local.start()
    arrived(span(left, 0, rows), recv.at[left])
    sent.append(push(span(left, 0, half), span(left, 0, half), len(sent), recv.at[left], right))
    arrived(span(right, 0, rows), recv.at[right])
    sent.append(push(span(right, half, half), span(right, half, half), len(sent), recv.at[right], left))
    for q in range(chunks):
        chunk = span(across, q * piece, piece)
        arrived(chunk, recv_z.at[q])
        sent.append(push(chunk, chunk, len(sent), recv.at[across], left))
        sent.append(push(chunk, chunk, len(sent), recv.at[across], right))
    left_across = (left + ring) % n_dp
    right_across = (right + ring) % n_dp
    arrived(span(left_across, 0, rows), recv.at[left_across])
    sent.append(
        push(span(left_across, 0, half), span(left_across, 0, half), len(sent), recv.at[left_across], right)
    )
    arrived(span(right_across, 0, rows), recv.at[right_across])
    sent.append(
        push(span(right_across, half, half), span(right_across, half, half), len(sent), recv.at[right_across], left)
    )
    arrived(span(far, 0, rows), recv.at[far])
    far_across = (far + ring) % n_dp
    arrived(span(far_across, 0, rows), recv.at[far_across])
    local.wait()
    for copy in sent:
        copy.wait_send()


def dp_gather(block):
    n_dp = lax.axis_size("dp")
    ring = n_dp // 2
    chunks = 4
    cap, rows, row_width = block.shape
    sends = 3 * chunks + 6
    return pl.pallas_call(
        functools.partial(dp_gather_kernel, n_dp, ring, chunks),
        out_shape=jax.ShapeDtypeStruct((cap, n_dp * rows, row_width), block.dtype),
        in_specs=[pl.BlockSpec(memory_space=pl.ANY)],
        out_specs=pl.BlockSpec(memory_space=pl.ANY),
        scratch_shapes=[
            pltpu.SemaphoreType.DMA((n_dp,)),
            pltpu.SemaphoreType.DMA((chunks,)),
            pltpu.SemaphoreType.DMA((sends,)),
            pltpu.VMEM(block.shape, block.dtype),
            pltpu.SemaphoreType.DMA((1,)),
        ],
        compiler_params=pltpu.CompilerParams(
            collective_id=0, has_side_effects=True, vmem_limit_bytes=32 * 1024 * 1024
        ),
    )(block)


def expert_exchange_kernel(n_ex, x_ref, o_ref, recv, send, local_sem):
    me = lax.axis_index("expert")
    dp = lax.axis_index("dp")
    barrier = pltpu.get_barrier_semaphore()
    for step in range(1, n_ex):
        peer = (me + step) % n_ex
        pl.semaphore_signal(barrier, inc=1, device_id=(dp, peer), device_id_type=pl.DeviceIdType.MESH)
    pl.semaphore_wait(barrier, n_ex - 1)
    local = pltpu.make_async_copy(x_ref.at[pl.ds(me, 1)], o_ref.at[pl.ds(me, 1)], local_sem.at[0])
    local.start()
    sent = []
    for step in range(1, n_ex):
        peer = (me + step) % n_ex
        copy = pltpu.make_async_remote_copy(
            src_ref=x_ref.at[pl.ds(peer, 1)],
            dst_ref=o_ref.at[pl.ds(me, 1)],
            send_sem=send.at[step],
            recv_sem=recv.at[0],
            device_id=(dp, peer),
            device_id_type=pl.DeviceIdType.MESH,
        )
        copy.start()
        sent.append(copy)
    pltpu.make_async_copy(
        x_ref.at[pl.ds(0, n_ex - 1)], o_ref.at[pl.ds(0, n_ex - 1)], recv.at[0]
    ).wait()
    local.wait()
    for copy in sent:
        copy.wait_send()


def expert_exchange(block):
    n_ex = lax.axis_size("expert")
    return pl.pallas_call(
        functools.partial(expert_exchange_kernel, n_ex),
        out_shape=jax.ShapeDtypeStruct(block.shape, block.dtype),
        in_specs=[pl.BlockSpec(memory_space=pl.ANY)],
        out_specs=pl.BlockSpec(memory_space=pl.ANY),
        scratch_shapes=[
            pltpu.SemaphoreType.DMA((1,)),
            pltpu.SemaphoreType.DMA((n_ex,)),
            pltpu.SemaphoreType.DMA((1,)),
        ],
        compiler_params=pltpu.CompilerParams(collective_id=1, has_side_effects=True),
    )(block)


def body(tokens, cotangent, expert_ids, gates, swap_flags, gate_w, up_w, down_w):
    axis_len = lax.axis_size("expert")
    half_axis = axis_len // 2
    pair_bit = axis_len.bit_length() - 2
    own_slot = lax.axis_index("expert")
    tok_count = tokens.shape[0]
    top_count = expert_ids.shape[1]
    width = tokens.shape[1]
    flat_ids = expert_ids.reshape(-1)
    choice_count = flat_ids.shape[0]
    valid = flat_ids < axis_len
    pair_index = jnp.arange(half_axis, dtype=jnp.int32)
    flag_of = jnp.sum(
        jnp.where((flat_ids % half_axis)[:, None] == pair_index[None, :], swap_flags[None, :], 0),
        axis=1,
    )
    own_flag = jnp.sum(jnp.where(pair_index == own_slot % half_axis, swap_flags, 0))
    target = jnp.where(flag_of == 1, jnp.bitwise_xor(flat_ids, half_axis), flat_ids)
    target = jnp.where(valid, target, 0)
    onehot = (
        (target[:, None] == jnp.arange(axis_len, dtype=jnp.int32)[None, :]) & valid[:, None]
    ).astype(jnp.bfloat16)
    order = jnp.arange(choice_count, dtype=jnp.int32)
    lower = (order[None, :] <= order[:, None]).astype(jnp.bfloat16)
    counts = jnp.dot(lower, onehot, preferred_element_type=jnp.float32)
    ranks = jnp.sum(counts * onehot.astype(jnp.float32), axis=1).astype(jnp.int32) - 1
    slot_count = axis_len * CAP
    slots = jnp.where(valid, target * CAP + ranks, slot_count)
    pick = (slots[:, None] == jnp.arange(slot_count, dtype=jnp.int32)[None, :]).astype(jnp.bfloat16)
    token_pick = jnp.sum(pick.reshape(tok_count, top_count, slot_count).astype(jnp.float32), axis=1)
    token_pick = token_pick.astype(jnp.bfloat16)
    rows_xdy = lax.dot_general(
        token_pick,
        jnp.concatenate([tokens, cotangent], axis=1),
        (((0,), (0,)), ((), ())),
        preferred_element_type=jnp.float32,
    ).astype(tokens.dtype)
    send_g = jnp.dot(gates.reshape(1, -1), pick, preferred_element_type=jnp.float32).astype(gates.dtype)
    g_cols = jnp.where(
        jnp.arange(LANE, dtype=jnp.int32)[None, :] == 0, send_g.reshape(-1, 1), jnp.zeros((), gates.dtype)
    )
    packed = jnp.concatenate([rows_xdy, g_cols], axis=1)
    row_width = packed.shape[1]
    packed = packed.reshape(axis_len, CAP * row_width // LANE, LANE)
    recv = expert_exchange(packed).reshape(axis_len, CAP, row_width)
    recv = jnp.transpose(recv, (1, 0, 2))
    recv, gate_w, up_w, down_w = lax.optimization_barrier((recv, gate_w, up_w, down_w))
    w_gate = gate_w[0]
    w_up = up_w[0]
    w_down = down_w[0]
    other_gate, other_up, other_down = partner((gate_w, up_w, down_w), "expert", pair_bit)
    taken = own_flag == 1
    w_gate = jnp.where(taken, other_gate[0], w_gate)
    w_up = jnp.where(taken, other_up[0], w_up)
    w_down = jnp.where(taken, other_down[0], w_down)
    gathered = dp_gather(recv)
    block_count = lax.axis_size("dp")
    row_x = gathered[:, :, :width]
    row_dy = gathered[:, :, width:2 * width]
    row_g = gathered[:, :, 2 * width:2 * width + 1]
    feature = (((2,), (0,)), ((), ()))
    rows_contract = (((0, 1), (0, 1)), ((), ()))
    hidden_count = w_gate.shape[1]
    w_both = jnp.concatenate([w_gate, w_up], axis=1)
    pre_both = lax.dot_general(row_x, w_both, feature, preferred_element_type=jnp.float32)
    pre_gate = pre_both[:, :, :hidden_count]
    pre_up = pre_both[:, :, hidden_count:]
    sigma = jax.nn.sigmoid(pre_gate)
    active = pre_gate * sigma
    hidden = (active * pre_up).astype(jnp.bfloat16)
    back = lax.dot_general(
        row_dy, w_down, (((2,), (1,)), ((), ())), preferred_element_type=jnp.float32
    )
    score = jnp.sum(hidden.astype(jnp.float32) * back, axis=2).T
    scaled = row_dy * row_g
    d_hidden = row_g.astype(jnp.float32) * back
    d_gate = (d_hidden * pre_up * sigma * (1.0 + pre_gate * (1.0 - sigma))).astype(jnp.bfloat16)
    d_up = (d_hidden * active).astype(jnp.bfloat16)
    d_both = jnp.concatenate([d_gate, d_up], axis=2)
    grad_both = lax.dot_general(row_x, d_both, rows_contract, preferred_element_type=jnp.float32)
    grad_gate = grad_both[:, :hidden_count]
    grad_up = grad_both[:, hidden_count:]
    grad_down = lax.dot_general(hidden, scaled, rows_contract, preferred_element_type=jnp.float32)
    scores = score.reshape(block_count, axis_len * CAP)
    parts = lax.all_to_all(scores, "dp", split_axis=0, concat_axis=0, tiled=True)
    own_scores = jnp.sum(parts, axis=0).reshape(axis_len, CAP)
    returned = lax.all_to_all(own_scores, "expert", split_axis=0, concat_axis=0, tiled=True)
    picked = jnp.sum(jnp.where(pick > 0, returned.reshape(1, -1), 0.0), axis=1)
    score_grad = jnp.where(valid, picked, 0.0).reshape(tok_count, top_count)
    out_gate = grad_gate.astype(jnp.bfloat16)[None]
    out_up = grad_up.astype(jnp.bfloat16)[None]
    out_down = grad_down.astype(jnp.bfloat16)[None]
    return (out_gate, out_up, out_down, score_grad)


def solution(mesh):
    placed = (
        P(("dp", "expert"), None),
        P(("dp", "expert"), None),
        P(("dp", "expert"), None),
        P(("dp", "expert"), None),
        P(),
        P("expert", None, "dp"),
        P("expert", None, "dp"),
        P("expert", "dp", None),
    )
    return jax.shard_map(
        body,
        mesh=mesh,
        in_specs=placed,
        out_specs=(
            P("expert", None, "dp"),
            P("expert", None, "dp"),
            P("expert", "dp", None),
            P(("dp", "expert"), None),
        ),
        check_vma=False,
    )
```
